256 devices in a mesh: row: 16 (over y, z_hi), col: 16 (over x, z_lo, core).
Axes of the slice: x: 4, y: 4, z: 8 (z_hi: 4, z_lo: 2; z = z_hi * 2 + z_lo), core: 2. Of those that a mesh axis runs over, the one named last changes fastest.
Arguments:
- feat_one: bfloat16 [32768, 128], P(('row', 'col')), may hold values from -16 to 16
- feat_two: bfloat16 [32768, 128], P(('col', 'row')), may hold values from -16 to 16
- value_one: bfloat16 [32768, 128], P(('row', 'col')), may hold values from -6 to 6
- value_two: bfloat16 [32768, 128], P(('col', 'row')), may hold values from -6 to 6
Outputs:
- matched_one: float32 [32768, 128], P(('row', 'col'))
- flow_one: float32 [2, 32768], P(None, ('row', 'col'))
- matched_two: float32 [32768, 128], P(('col', 'row'))
- flow_two: float32 [2, 32768], P(None, ('col', 'row'))
The draws below stay inside these ranges and needn't reach their ends.
All inputs are finite; a program needn't handle non-finite values.
Results may differ from the reference program's by a relative error of at most 0.0011.
Values may be sent and summed in bfloat16 or wider, within the bound.
No kernel may reach another device: no remote copies, remote signals or barrier semaphores. Data moves between devices by JAX's collectives and lax.ppermute only.
A program may use at most 128 MiB of HBM per device.

```python
import math
import jax
import jax.numpy as jnp
from jax import lax

FEAT = 128
GRID_W = 256
TOKENS = 32768
BLK = 512


def normal_features(key, salt):
    own = jax.random.fold_in(key, salt)
    key_noise, key_scale = jax.random.split(own)
    scales = jnp.exp(jax.random.uniform(key_scale, (TOKENS, 1), jnp.float32, math.log(0.8), math.log(3.0)))
    raw = jax.random.normal(key_noise, (TOKENS, FEAT), jnp.float32) * scales
    return jnp.clip(raw, -16.0, 16.0)


def draw_feat_one(key, part):
    raw = normal_features(key, 1103)
    return raw.astype(jnp.bfloat16)


def draw_feat_two(key, part):
    raw = normal_features(key, 2207)
    return raw.astype(jnp.bfloat16)


def levels(rng, shape, shards, smallest, largest):
    factor_of = 1.0
    for axis_at, blocks in shards:
        draws = jax.random.uniform(jax.random.fold_in(jax.random.fold_in(rng, 6), axis_at), (blocks,), jnp.float32, smallest / len(shards), largest / len(shards))
        factor_of = factor_of * jnp.repeat(jnp.exp(draws), shape[axis_at] // blocks).reshape((-1,) + (1,) * (len(shape) - 1 - axis_at))
    return factor_of


def gaussian(key, dims, spread, most, cuts=(), kind=jnp.bfloat16):
    drawn = spread * jax.random.normal(key, dims, jnp.float32)
    if cuts:
        drawn = drawn * levels(key, dims, cuts, -0.22, 0.18)
    return jnp.clip(drawn, -most, most).astype(kind)


def setup_inputs(seed: int = 0) -> dict:
    key_of = jax.random.split(jax.random.key(seed), 5)
    return {
        "feat_one": draw_feat_one(jax.random.fold_in(key_of[4], 71), 0),
        "feat_two": draw_feat_two(jax.random.fold_in(key_of[4], 71), 0),
        "value_one": gaussian(key_of[2], (TOKENS, FEAT), 1.0, 6.0, ((0, 256),)),
        "value_two": gaussian(key_of[3], (TOKENS, FEAT), 1.0, 6.0, ((0, 256),)),
    }


def token_coords(start, count, total):
    index = start + lax.iota(jnp.int32, count)
    across = (index % GRID_W).astype(jnp.float32) / GRID_W
    down = (index // GRID_W).astype(jnp.float32) / (total // GRID_W)
    return (across, down)

def flash_merge(first, second):
    peak_a, total_a, acc_a, across_a, down_a = first
    peak_b, total_b, acc_b, across_b, down_b = second
    peak = jnp.maximum(peak_a, peak_b)
    factor_a = jnp.exp(peak_a - peak)
    factor_b = jnp.exp(peak_b - peak)
    return (peak, total_a * factor_a + total_b * factor_b, acc_a * factor_a[:, None] + acc_b * factor_b[:, None], across_a * factor_a + across_b * factor_b, down_a * factor_a + down_b * factor_b)

def reference(feat_one, feat_two, value_one, value_two):
    scale = 1.0 / math.sqrt(FEAT)
    blocks = TOKENS // BLK
    all_across, all_down = token_coords(0, TOKENS, TOKENS)
    across_blocks = all_across.reshape(blocks, BLK)
    down_blocks = all_down.reshape(blocks, BLK)
    value_blocks = value_two.astype(jnp.float32).reshape(blocks, BLK, FEAT)

    def sweep(carry, block_index):
        start = (block_index * BLK).astype(jnp.int32)
        rows_feat = lax.dynamic_slice_in_dim(feat_one, start, BLK, 0)
        rows_value = lax.dynamic_slice_in_dim(value_one, start, BLK, 0)
        rows_across, rows_down = token_coords(start, BLK, TOKENS)
        scores = lax.dot_general(rows_feat, feat_two, (((1,), (1,)), ((), ())), preferred_element_type=jnp.float32) * scale
        tiled = scores.reshape(BLK, blocks, BLK)
        row_peak = lax.optimization_barrier(jnp.max(tiled, axis=2))
        row_weight = jnp.exp(tiled - row_peak[:, :, None]).astype(jnp.bfloat16)
        weight_f = row_weight.astype(jnp.float32)
        part_total = lax.optimization_barrier(jnp.sum(weight_f, axis=2))
        part_across = lax.optimization_barrier(jnp.sum(weight_f * across_blocks[None], axis=2))
        part_down = lax.optimization_barrier(jnp.sum(weight_f * down_blocks[None], axis=2))
        part_acc = jnp.einsum('rkt,ktc->rkc', weight_f, value_blocks)
        row_top = lax.optimization_barrier(jnp.max(row_peak, axis=1))
        factor = jnp.exp(row_peak - row_top[:, None])
        row_out = (row_top, lax.optimization_barrier(jnp.sum(factor * part_total, axis=1)), lax.optimization_barrier(jnp.sum(factor[:, :, None] * part_acc, axis=1)), lax.optimization_barrier(jnp.sum(factor * part_across, axis=1)), lax.optimization_barrier(jnp.sum(factor * part_down, axis=1)))
        col_peak = lax.optimization_barrier(jnp.max(scores, axis=0))
        col_weight = jnp.exp(scores - col_peak[None]).astype(jnp.bfloat16)
        cweight_f = col_weight.astype(jnp.float32)
        col_acc = jnp.dot(cweight_f.T, rows_value.astype(jnp.float32), precision=lax.Precision.HIGHEST)
        col_part = (col_peak, lax.optimization_barrier(jnp.sum(cweight_f, axis=0)), col_acc, lax.optimization_barrier(jnp.sum(cweight_f * rows_across[:, None], axis=0)), lax.optimization_barrier(jnp.sum(cweight_f * rows_down[:, None], axis=0)))
        return (flash_merge(carry, col_part), row_out)
    init = (jnp.full((TOKENS,), -jnp.inf, jnp.float32), jnp.zeros((TOKENS,), jnp.float32), jnp.zeros((TOKENS, FEAT), jnp.float32), jnp.zeros((TOKENS,), jnp.float32), jnp.zeros((TOKENS,), jnp.float32))
    carry, row_out = lax.scan(sweep, init, jnp.arange(blocks, dtype=jnp.int32))
    row_total = row_out[1].reshape(TOKENS)
    row_acc = row_out[2].reshape(TOKENS, FEAT)
    row_across = row_out[3].reshape(TOKENS)
    row_down = row_out[4].reshape(TOKENS)
    matched_one = row_acc / row_total[:, None]
    flow_one = jnp.stack([row_across / row_total - all_across, row_down / row_total - all_down])
    col_total, col_acc, col_across, col_down = (carry[1], carry[2], carry[3], carry[4])
    matched_two = col_acc / col_total[:, None]
    flow_two = jnp.stack([col_across / col_total - all_across, col_down / col_total - all_down])
    return (matched_one, flow_one, matched_two, flow_two)
```

```python
import math

import jax
import jax.numpy as jnp
from jax import lax
from jax.experimental import pallas as pl
from jax.experimental.pallas import tpu as pltpu
from jax.sharding import PartitionSpec as P

GRID_W = 256
SUB = 4
SHARD = 128
WIDTH = 128
BLOCK = SUB * SHARD
ROWS = WIDTH + 8
AUG = WIDTH + 16
TOTAL_ROW, ACROSS_ROW, DOWN_ROW, PEAK_ROW = 0, 1, 2, 3
VMEM = pl.BlockSpec(memory_space=pltpu.VMEM)


def slow_shift(axis, value, step):
    pairs = [(i, ((i // SUB + step) % SUB) * SUB + i % SUB) for i in range(SUB * SUB)]
    return lax.ppermute(value, axis, pairs)


def fast_shift(axis, value, step):
    pairs = [(i, (i // SUB) * SUB + (i % SUB + step) % SUB) for i in range(SUB * SUB)]
    return lax.ppermute(value, axis, pairs)


def fast_swap(axis, value, step):
    return lax.ppermute(value, axis, [(i, i ^ step) for i in range(SUB * SUB)])


def pack_kernel(feat_one, value_one, feat_two, value_two, out_one, out_two):
    for feat, value, out in ((feat_one, value_one, out_one), (feat_two, value_two, out_two)):
        out[:, :WIDTH] = feat[...]
        out[:, WIDTH:] = value[...].astype(jnp.float32).T.astype(jnp.bfloat16)


def piece_coords(start, total):
    across = (start % GRID_W).astype(jnp.float32) / GRID_W
    down = (start // GRID_W).astype(jnp.float32) / (total // GRID_W)
    return across, down


def score_kernel(total, scale, *refs):
    ins, outs, (feats, values, acc) = refs[:8], refs[8:16], refs[16:]
    row, col = lax.axis_index("row"), lax.axis_index("col")
    sub = lax.broadcasted_iota(jnp.int32, (AUG - WIDTH, SHARD), 0)
    lane = lax.broadcasted_iota(jnp.int32, (AUG - WIDTH, SHARD), 1).astype(jnp.float32) / GRID_W
    for side in range(2):
        group, member = (row, col) if side == 0 else (col, row)
        for block in range(SUB):
            source = ins[side * SUB + block]
            slow = (member // SUB + block) % SUB
            for piece in range(SUB):
                fast = member % SUB
                fast = fast ^ piece if side == 0 else (fast + piece) % SUB
                start = ((group * SUB + slow) * SUB + fast) * SHARD
                across, down = piece_coords(start, total)
                extra = jnp.where(sub == DOWN_ROW, down, 0.0)
                extra = jnp.where(sub == ACROSS_ROW, across + lane, extra)
                extra = jnp.where(sub == TOTAL_ROW, 1.0, extra)
                span = slice(piece * SHARD, (piece + 1) * SHARD)
                feats[side * SUB + block, span, :] = source[piece, :, :WIDTH]
                values[side * SUB + block, :WIDTH, span] = source[piece, :, WIDTH:]
                values[side * SUB + block, WIDTH:, span] = extra.astype(jnp.bfloat16)

    def step(index, _):
        other = (1 - index // SUB) * SUB
        query = feats[index]
        peaks, parts = [], []
        for block in range(SUB):
            score = lax.dot_general(
                feats[other + block], query, (((1,), (1,)), ((), ())),
                preferred_element_type=jnp.float32,
            ) * scale
            peak = jnp.max(score, axis=0, keepdims=True)
            weight = jnp.exp2(score - peak).astype(jnp.bfloat16)
            parts.append(
                jnp.dot(values[other + block], weight, preferred_element_type=jnp.float32)[:ROWS]
            )
            peaks.append(peak)
        store_merged(acc.at[index], peaks, parts)
        return 0

    lax.fori_loop(0, 2 * SUB, step, 0)
    for index in range(2 * SUB):
        outs[index][...] = acc[index]


def merge(peaks, parts):
    top = peaks[0]
    for peak in peaks[1:]:
        top = jnp.maximum(top, peak)
    whole = None
    for peak, part in zip(peaks, parts):
        term = part * jnp.exp2(peak - top)
        whole = term if whole is None else whole + term
    return top, whole


def store_merged(out, peaks, parts):
    top, whole = merge(peaks, parts)
    sub = lax.broadcasted_iota(jnp.int32, (ROWS - WIDTH, top.shape[1]), 0)
    out[:WIDTH, :] = whole[:WIDTH]
    out[WIDTH:, :] = jnp.where(sub == PEAK_ROW, top, whole[WIDTH:])


def peak_of(part):
    return part[WIDTH + PEAK_ROW : WIDTH + PEAK_ROW + 1, :]


def merge_kernel(*refs):
    ins, outs = refs[: 2 * SUB], refs[2 * SUB :]
    for side in range(2):
        for piece in range(SUB):
            span = slice(piece * SHARD, (piece + 1) * SHARD)
            parts = [ref[:, span] for ref in ins[side * SUB : (side + 1) * SUB]]
            store_merged(outs[side * SUB + piece], [peak_of(part) for part in parts], parts)


def finish_kernel(total, *refs):
    ins, outs = refs[: 2 * SUB], refs[2 * SUB :]
    row, col = lax.axis_index("row"), lax.axis_index("col")
    lane = lax.broadcasted_iota(jnp.int32, (1, SHARD), 1).astype(jnp.float32) / GRID_W
    for side in range(2):
        group, member = (row, col) if side == 0 else (col, row)
        own_across, own_down = piece_coords((group * SUB * SUB + member) * SHARD, total)
        parts = [ref[...] for ref in ins[side * SUB : (side + 1) * SUB]]
        _, whole = merge([peak_of(part) for part in parts], parts)
        inverse = 1.0 / whole[WIDTH + TOTAL_ROW : WIDTH + TOTAL_ROW + 1, :]
        matched, flow = outs[2 * side], outs[2 * side + 1]
        matched[...] = (whole[:WIDTH] * inverse).T
        across = whole[WIDTH + ACROSS_ROW : WIDTH + ACROSS_ROW + 1, :] * inverse
        down = whole[WIDTH + DOWN_ROW : WIDTH + DOWN_ROW + 1, :] * inverse
        flow[0:1, :] = across - (own_across + lane)
        flow[1:2, :] = down - own_down


def call(kernel, shapes, args, scratch=(), cost=None):
    return pl.pallas_call(
        kernel,
        out_shape=shapes,
        in_specs=[VMEM] * len(args),
        out_specs=[VMEM] * len(shapes),
        scratch_shapes=list(scratch),
        compiler_params=pltpu.CompilerParams(vmem_limit_bytes=48 << 20),
        cost_estimate=cost,
    )(*args)


def body(feat_one, feat_two, value_one, value_two):
    total = feat_one.shape[0] * lax.axis_size("row") * lax.axis_size("col")
    scale = math.log2(math.e) / math.sqrt(WIDTH)
    packed = jax.ShapeDtypeStruct((SHARD, 2 * WIDTH), jnp.bfloat16)
    own_one, own_two = call(
        pack_kernel, [packed] * 2, (feat_one, value_one, feat_two, value_two)
    )
    one = [own_one] + [fast_swap("col", own_one, step) for step in range(1, SUB)]
    two = [own_two] + [fast_shift("row", own_two, -step) for step in range(1, SUB)]
    one, two = jnp.stack(one), jnp.stack(two)
    ones = [one] + [slow_shift("col", one, -step) for step in range(1, SUB)]
    twos = [two] + [slow_shift("row", two, -step) for step in range(1, SUB)]

    def score(*refs):
        score_kernel(total, scale, *refs)

    def finish(*refs):
        finish_kernel(total, *refs)

    wide = jax.ShapeDtypeStruct((ROWS, BLOCK), jnp.float32)
    narrow = jax.ShapeDtypeStruct((ROWS, SHARD), jnp.float32)
    parts = call(
        score,
        [wide] * (2 * SUB),
        (*ones, *twos),
        scratch=[
            pltpu.VMEM((2 * SUB, BLOCK, WIDTH), jnp.bfloat16),
            pltpu.VMEM((2 * SUB, AUG, BLOCK), jnp.bfloat16),
            pltpu.VMEM((2 * SUB, ROWS, BLOCK), jnp.float32),
        ],
    )
    rows, cols = parts[:SUB], parts[SUB:]
    rows = [rows[0]] + [slow_shift("col", rows[step], step) for step in range(1, SUB)]
    cols = [cols[0]] + [slow_shift("row", cols[step], step) for step in range(1, SUB)]
    parts = call(merge_kernel, [narrow] * (2 * SUB), (*rows, *cols))
    rows, cols = parts[:SUB], parts[SUB:]
    rows = [rows[0]] + [fast_swap("col", rows[step], step) for step in range(1, SUB)]
    cols = [cols[0]] + [fast_shift("row", cols[step], step) for step in range(1, SUB)]
    matched = jax.ShapeDtypeStruct((SHARD, WIDTH), jnp.float32)
    flow = jax.ShapeDtypeStruct((2, SHARD), jnp.float32)
    return tuple(call(finish, [matched, flow] * 2, (*rows, *cols)))


def solution(mesh):
    return jax.shard_map(
        body,
        mesh=mesh,
        in_specs=(
            P(("row", "col"), None),
            P(("col", "row"), None),
            P(("row", "col"), None),
            P(("col", "row"), None),
        ),
        out_specs=(
            P(("row", "col"), None),
            P(None, ("row", "col")),
            P(("col", "row"), None),
            P(None, ("col", "row")),
        ),
        check_vma=False,
    )
```

```python
import functools
import math

import jax
import jax.numpy as jnp
from jax import lax
from jax.experimental import pallas as pl
from jax.experimental.pallas import tpu as pltpu
from jax.sharding import PartitionSpec as P

GRID_W = 256
SUB = 4
SHARD = 128
WIDTH = 128
BLOCK = SUB * SHARD
ROWS = WIDTH + 8
AUG = 16
TOTAL_ROW, ACROSS_ROW, DOWN_ROW, PEAK_ROW = 0, 1, 2, 3
VMEM = pl.BlockSpec(memory_space=pltpu.VMEM)
HBM = pl.BlockSpec(memory_space=pltpu.HBM)


def slow_shift(axis, value, step):
    pairs = [(i, ((i // SUB + step) % SUB) * SUB + i % SUB) for i in range(SUB * SUB)]
    return lax.ppermute(value, axis, pairs)


def fast_shift(axis, value, step):
    pairs = [(i, (i // SUB) * SUB + (i % SUB + step) % SUB) for i in range(SUB * SUB)]
    return lax.ppermute(value, axis, pairs)


def fast_swap(axis, value, step):
    return lax.ppermute(value, axis, [(i, i ^ step) for i in range(SUB * SUB)])


def pack_kernel(feat_one, value_one, feat_two, value_two, out_one, out_two, held, sems):
    copies = [
        pltpu.make_async_copy(feat_one, out_one.at[:, :WIDTH], sems.at[0]),
        pltpu.make_async_copy(feat_two, out_two.at[:, :WIDTH], sems.at[1]),
        pltpu.make_async_copy(value_one, held.at[0], sems.at[2]),
        pltpu.make_async_copy(value_two, held.at[1], sems.at[3]),
    ]
    for copy in copies:
        copy.start()
    for side, out in ((0, out_one), (1, out_two)):
        copies[2 + side].wait()
        out[:, WIDTH:] = held[side].astype(jnp.float32).T.astype(jnp.bfloat16)
    copies[0].wait()
    copies[1].wait()


def piece_coords(start, total):
    across = (start % GRID_W).astype(jnp.float32) / GRID_W
    down = (start // GRID_W).astype(jnp.float32) / (total // GRID_W)
    return across, down


def coord_rows(start, total):
    across, down = piece_coords(start, total)
    sub = lax.broadcasted_iota(jnp.int32, (AUG, SHARD), 0)
    lane = lax.broadcasted_iota(jnp.int32, (AUG, SHARD), 1).astype(jnp.float32) / GRID_W
    rows = jnp.where(sub == DOWN_ROW, down, 0.0)
    rows = jnp.where(sub == ACROSS_ROW, across + lane, rows)
    rows = jnp.where(sub == TOTAL_ROW, 1.0, rows)
    return rows.astype(jnp.bfloat16)


def block_of(pieces, starts, total):
    keys = jnp.concatenate([piece[:, :WIDTH] for piece in pieces], axis=0)
    values = jnp.concatenate([piece[:, WIDTH:] for piece in pieces], axis=1)
    extra = jnp.concatenate([coord_rows(start, total) for start in starts], axis=1)
    return keys, jnp.concatenate([values, extra], axis=0)


def start_one(slow, fast_high, fast_low):
    row, col = lax.axis_index("row"), lax.axis_index("col")
    x = (col // SUB + slow) % SUB
    fast = (col % SUB) ^ (2 * fast_high + fast_low)
    return ((row * SUB + x) * SUB + fast) * SHARD


def start_two(slow, fast):
    row, col = lax.axis_index("row"), lax.axis_index("col")
    y = (row // SUB + slow) % SUB
    z = (row % SUB + fast) % SUB
    return ((col * SUB + y) * SUB + z) * SHARD


def merge(peaks, parts):
    top = peaks[0]
    for peak in peaks[1:]:
        top = jnp.maximum(top, peak)
    whole = None
    for peak, part in zip(peaks, parts):
        term = part * jnp.exp2(peak - top)
        whole = term if whole is None else whole + term
    return top, whole


def with_peak(top, whole):
    sub = lax.broadcasted_iota(jnp.int32, (ROWS - WIDTH, top.shape[1]), 0)
    return jnp.concatenate(
        [whole[:WIDTH], jnp.where(sub == PEAK_ROW, top, whole[WIDTH:])], axis=0
    )


def peak_of(part):
    return part[WIDTH + PEAK_ROW : WIDTH + PEAK_ROW + 1, :]


def merged(parts):
    return with_peak(*merge([peak_of(part) for part in parts], parts))


def attend(scale, query, blocks):
    peaks, parts = [], []
    for keys, values in blocks:
        score = lax.dot_general(
            keys, query, (((1,), (1,)), ((), ())), preferred_element_type=jnp.float32
        ) * scale
        peak = jnp.max(score, axis=0, keepdims=True)
        weight = jnp.exp2(score - peak).astype(jnp.bfloat16)
        parts.append(jnp.dot(values, weight, preferred_element_type=jnp.float32)[:ROWS])
        peaks.append(peak)
    return with_peak(*merge(peaks, parts))


def one_block(ones, slow, total):
    pieces = [ones[low * 2 + high][slow] for low in range(2) for high in range(2)]
    starts = [start_one(slow, high, low) for low in range(2) for high in range(2)]
    return block_of(pieces, starts, total)


def two_block(two, slow, total):
    return block_of(
        [two[piece] for piece in range(SUB)],
        [start_two(slow, piece) for piece in range(SUB)],
        total,
    )


def col_kernel(total, scale, *refs):
    ones, two, out = refs[:SUB], refs[SUB], refs[SUB + 1]
    query = jnp.concatenate([two[piece, :, :WIDTH] for piece in range(SUB)], axis=0)
    out[...] = attend(scale, query, [one_block(ones, slow, total) for slow in range(SUB)])


def row_kernel(total, scale, first, *refs):
    ones, twos, (keep, send) = refs[:SUB], refs[SUB : 2 * SUB], refs[2 * SUB :]

    def step(slow, _):
        query = jnp.concatenate([ref[first + slow, :, :WIDTH] for ref in ones], axis=0)
        blocks = [two_block(two, block, total) for block, two in enumerate(twos)]
        whole = attend(scale, query, blocks)
        keep[slow] = whole[:, : BLOCK // 2]
        send[slow] = whole[:, BLOCK // 2 :]
        return 0

    lax.fori_loop(0, keep.shape[0], step, 0)


def halve_kernel(mine, theirs, mine_b, theirs_b, keep, send):
    half = SUB // 2
    for slow in range(half):
        for first, one, two in ((0, mine, theirs), (half, mine_b, theirs_b)):
            whole = merged([one[slow], two[slow]])
            keep[first + slow] = whole[:, :SHARD]
            send[first + slow] = whole[:, SHARD:]


def pair_kernel(mine, theirs, *outs):
    for slow in range(SUB):
        outs[slow][...] = merged([mine[slow], theirs[slow]])


def block_kernel(*refs):
    ins, outs = refs[:SUB], refs[SUB:]
    for piece in range(SUB):
        span = slice(piece * SHARD, (piece + 1) * SHARD)
        outs[piece][...] = merged([ref[:, span] for ref in ins])


def finish_kernel(total, own_start, *refs):
    ins, (matched, flow) = refs[:SUB], refs[SUB:]
    own_across, own_down = piece_coords(own_start(), total)
    lane = lax.broadcasted_iota(jnp.int32, (1, SHARD), 1).astype(jnp.float32) / GRID_W
    parts = [ref[...] for ref in ins]
    _, whole = merge([peak_of(part) for part in parts], parts)
    inverse = 1.0 / whole[WIDTH + TOTAL_ROW : WIDTH + TOTAL_ROW + 1, :]
    matched[...] = (whole[:WIDTH] * inverse).T
    across = whole[WIDTH + ACROSS_ROW : WIDTH + ACROSS_ROW + 1, :] * inverse
    down = whole[WIDTH + DOWN_ROW : WIDTH + DOWN_ROW + 1, :] * inverse
    flow[0:1, :] = across - (own_across + lane)
    flow[1:2, :] = down - own_down


def call(kernel, shapes, args, scratch=(), work=0, specs=None, vmem=48 << 20):
    moved = sum(math.prod(a.shape) * a.dtype.itemsize for a in (*args, *shapes))
    return pl.pallas_call(
        kernel,
        out_shape=shapes,
        in_specs=specs or [VMEM] * len(args),
        out_specs=[VMEM] * len(shapes),
        scratch_shapes=list(scratch),
        compiler_params=pltpu.CompilerParams(vmem_limit_bytes=vmem),
        cost_estimate=pl.CostEstimate(
            flops=4 * WIDTH * work, bytes_accessed=moved, transcendentals=work
        ),
    )(*args)


def together(values):
    return lax.optimization_barrier(values)


def f32(*shape):
    return jax.ShapeDtypeStruct(shape, jnp.float32)


def body(feat_one, feat_two, value_one, value_two):
    total = feat_one.shape[0] * lax.axis_size("row") * lax.axis_size("col")
    scale = math.log2(math.e) / math.sqrt(WIDTH)
    packed = jax.ShapeDtypeStruct((SHARD, 2 * WIDTH), jnp.bfloat16)
    own_one, own_two = call(
        pack_kernel,
        [packed] * 2,
        (feat_one, value_one, feat_two, value_two),
        scratch=[
            pltpu.VMEM((2, SHARD, WIDTH), jnp.bfloat16),
            pltpu.SemaphoreType.DMA((4,)),
        ],
        specs=[HBM] * 4,
        vmem=62 << 20,
    )

    two = [own_two] + [fast_shift("row", own_two, -step) for step in range(1, SUB)]
    one = [own_one, fast_swap("col", own_one, 2)]
    one, two = together((jnp.stack(one), jnp.stack(two)))
    one = [one] + [slow_shift("col", one, -step) for step in range(1, SUB)]
    near, far = slow_shift("row", two, -1), slow_shift("row", two, 1)
    one, near, far = together((jnp.stack(one, axis=1), near, far))
    twos = [two, near, slow_shift("row", two, -2), far]
    other = fast_swap("col", one, 1)
    ones = [one[0], one[1], other[0], other[1]]

    def col_scores(*refs):
        col_kernel(total, scale, *refs)

    def row_scores_of(first):
        return functools.partial(row_kernel, total, scale, first)

    def finish_one(*refs):
        finish_kernel(total, lambda: start_one(0, 0, 0), *refs)

    def finish_two(*refs):
        finish_kernel(total, lambda: start_two(0, 0), *refs)

    work = BLOCK * BLOCK * SUB
    cols = [None] * SUB
    for step in (0, 1, 3, 2):
        if step == 2:
            twos[2], _ = together((twos[2], cols[0]))
        (cols[step],) = call(col_scores, [f32(ROWS, BLOCK)], (*ones, twos[step]), work=work)
    ones, _ = together((ones, cols))
    cols = [cols[0]] + [slow_shift("row", cols[step], step) for step in range(1, SUB)]
    half = SUB // 2
    shapes = [f32(half, ROWS, BLOCK // 2)] * 2
    keep, send = call(row_scores_of(0), shapes, (*ones, *twos), work=half * work)
    theirs = fast_swap("col", send, 1)
    ones, cols, keep = together((ones, cols, keep))
    keep_b, send_b = call(row_scores_of(half), shapes, (*ones, *twos), work=half * work)
    theirs_b = fast_swap("col", send_b, 1)
    cols = call(block_kernel, [f32(ROWS, SHARD)] * SUB, cols)
    cols = [cols[0]] + [fast_shift("row", cols[step], step) for step in range(1, SUB)]
    keep, send = call(
        halve_kernel, [f32(SUB, ROWS, SHARD)] * 2, (keep, theirs, keep_b, theirs_b)
    )
    theirs = fast_swap("col", send, 2)
    rows = call(pair_kernel, [f32(ROWS, SHARD)] * SUB, (keep, theirs))
    rows = [rows[0]] + [slow_shift("col", rows[step], step) for step in range(1, SUB)]
    outs = [f32(SHARD, WIDTH), f32(2, SHARD)]
    matched_two, flow_two = call(finish_two, outs, cols)
    matched_one, flow_one = call(finish_one, outs, rows)
    return matched_one, flow_one, matched_two, flow_two


def solution(mesh):
    return jax.shard_map(
        body,
        mesh=mesh,
        in_specs=(
            P(("row", "col"), None),
            P(("col", "row"), None),
            P(("row", "col"), None),
            P(("col", "row"), None),
        ),
        out_specs=(
            P(("row", "col"), None),
            P(None, ("row", "col")),
            P(("col", "row"), None),
            P(None, ("col", "row")),
        ),
        check_vma=False,
    )
```

```python
import functools
import math

import jax
import jax.numpy as jnp
from jax import lax
from jax.experimental import pallas as pl
from jax.experimental.pallas import tpu as pltpu
from jax.sharding import PartitionSpec as P

GRID_W = 256
SUB = 4
SHARD = 128
WIDTH = 128
BLOCK = SUB * SHARD
ROWS = WIDTH + 8
AUG = 16
TOTAL_ROW, ACROSS_ROW, DOWN_ROW, PEAK_ROW = 0, 1, 2, 3
VMEM = pl.BlockSpec(memory_space=pltpu.VMEM)
HBM = pl.BlockSpec(memory_space=pltpu.HBM)


def slow_shift(axis, value, step):
    pairs = [(i, ((i // SUB + step) % SUB) * SUB + i % SUB) for i in range(SUB * SUB)]
    return lax.ppermute(value, axis, pairs)


def fast_shift(axis, value, step):
    pairs = [(i, (i // SUB) * SUB + (i % SUB + step) % SUB) for i in range(SUB * SUB)]
    return lax.ppermute(value, axis, pairs)


def fast_swap(axis, value, step):
    return lax.ppermute(value, axis, [(i, i ^ step) for i in range(SUB * SUB)])


def pack_kernel(feat_one, value_one, feat_two, value_two, out, feats, held, sems):
    sources = ((feat_one, value_one), (feat_two, value_two))
    copies = []
    for side, (feat, value) in enumerate(sources):
        copies.append(pltpu.make_async_copy(value, held.at[side], sems.at[2 * side]))
        copies.append(pltpu.make_async_copy(feat, feats.at[side], sems.at[2 * side + 1]))
    for copy in copies:
        copy.start()
    for side in range(2):
        copies[2 * side].wait()
        out[side, 1] = held[side].astype(jnp.float32).T.astype(jnp.bfloat16)
        copies[2 * side + 1].wait()
        out[side, 0] = feats[side]


def piece_coords(start, total):
    across = (start % GRID_W).astype(jnp.float32) / GRID_W
    down = (start // GRID_W).astype(jnp.float32) / (total // GRID_W)
    return across, down


def coord_rows(start, total):
    across, down = piece_coords(start, total)
    sub = lax.broadcasted_iota(jnp.int32, (AUG, SHARD), 0)
    lane = lax.broadcasted_iota(jnp.int32, (AUG, SHARD), 1).astype(jnp.float32) / GRID_W
    rows = jnp.where(sub == DOWN_ROW, down, 0.0)
    rows = jnp.where(sub == ACROSS_ROW, across + lane, rows)
    rows = jnp.where(sub == TOTAL_ROW, 1.0, rows)
    return rows.astype(jnp.bfloat16)


def key_start(side, slow, fast):
    row, col = lax.axis_index("row"), lax.axis_index("col")
    z = (row % SUB + fast) % SUB
    if side == 0:
        y = (row // SUB + slow) % SUB
        return ((col * SUB + y) * SUB + z) * SHARD
    x = (col // SUB + slow) % SUB
    return (((row // SUB * SUB + z) * SUB + x) * SUB + col % SUB) * SHARD


def own_start(side):
    row, col = lax.axis_index("row"), lax.axis_index("col")
    return (row * SUB * SUB + col if side == 0 else col * SUB * SUB + row) * SHARD


def merge(peaks, parts):
    top = peaks[0]
    for peak in peaks[1:]:
        top = jnp.maximum(top, peak)
    whole = None
    for peak, part in zip(peaks, parts):
        term = part * jnp.exp2(peak - top)
        whole = term if whole is None else whole + term
    return top, whole


def with_peak(top, whole):
    sub = lax.broadcasted_iota(jnp.int32, (ROWS - WIDTH, top.shape[1]), 0)
    return jnp.concatenate(
        [whole[:WIDTH], jnp.where(sub == PEAK_ROW, top, whole[WIDTH:])], axis=0
    )


def peak_of(part):
    return part[WIDTH + PEAK_ROW : WIDTH + PEAK_ROW + 1, :]


def merged(parts):
    return with_peak(*merge([peak_of(part) for part in parts], parts))


def attend(scale, query, blocks):
    peaks, parts = [], []
    for keys, values in blocks:
        score = lax.dot_general(
            keys, query, (((1,), (1,)), ((), ())), preferred_element_type=jnp.float32
        ) * scale
        peak = jnp.max(score, axis=0, keepdims=True)
        weight = jnp.exp2(score - peak).astype(jnp.bfloat16)
        parts.append(jnp.dot(values, weight, preferred_element_type=jnp.float32)[:ROWS])
        peaks.append(peak)
    return with_peak(*merge(peaks, parts))


def score_kernel(total, scale, side, first, queries, *refs):
    keys, (out,) = refs[:SUB], refs[SUB:]

    def block_of(slow):
        tiles = keys[slow]
        feats = jnp.concatenate([tiles[2 * fast] for fast in range(SUB)], axis=0)
        values = jnp.concatenate([tiles[2 * fast + 1] for fast in range(SUB)], axis=1)
        extra = [coord_rows(key_start(side, slow, fast), total) for fast in range(SUB)]
        return feats, jnp.concatenate([values, jnp.concatenate(extra, axis=1)], axis=0)

    def step(part, _):
        tiles = [queries[first + part * SUB + piece] for piece in range(SUB)]
        query = jnp.concatenate(tiles, axis=0)
        out[part] = attend(scale, query, [block_of(slow) for slow in range(SUB)])
        return 0

    lax.fori_loop(0, 2, step, 0)


def core_kernel(mine, theirs, *outs):
    for part in range(2):
        whole = merged([mine[part], theirs[part]])
        outs[2 * part][...] = whole[:, : 2 * SHARD]
        outs[2 * part + 1][...] = whole[:, 2 * SHARD :]


def chip_kernel(*refs):
    ins, (keep, send) = refs[: 2 * SUB], refs[2 * SUB :]
    for side in range(2):
        whole = merged([ref[...] for ref in ins[side * SUB : (side + 1) * SUB]])
        keep[side] = whole[:, :SHARD]
        send[side] = whole[:, SHARD:]


def finish_kernel(total, mine, theirs, *outs):
    lane = lax.broadcasted_iota(jnp.int32, (1, SHARD), 1).astype(jnp.float32) / GRID_W
    for side in range(2):
        matched, flow = outs[2 * side], outs[2 * side + 1]
        own_across, own_down = piece_coords(own_start(side), total)
        parts = [mine[side], theirs[side]]
        _, whole = merge([peak_of(part) for part in parts], parts)
        inverse = 1.0 / whole[WIDTH + TOTAL_ROW : WIDTH + TOTAL_ROW + 1, :]
        matched[...] = (whole[:WIDTH] * inverse).T
        across = whole[WIDTH + ACROSS_ROW : WIDTH + ACROSS_ROW + 1, :] * inverse
        down = whole[WIDTH + DOWN_ROW : WIDTH + DOWN_ROW + 1, :] * inverse
        flow[0:1, :] = across - (own_across + lane)
        flow[1:2, :] = down - own_down


def call(kernel, shapes, args, scratch=(), work=0, specs=None, vmem=48 << 20):
    moved = sum(math.prod(a.shape) * a.dtype.itemsize for a in (*args, *shapes))
    return pl.pallas_call(
        kernel,
        out_shape=shapes,
        in_specs=specs or [VMEM] * len(args),
        out_specs=[VMEM] * len(shapes),
        scratch_shapes=list(scratch),
        compiler_params=pltpu.CompilerParams(vmem_limit_bytes=vmem),
        cost_estimate=pl.CostEstimate(
            flops=4 * WIDTH * work, bytes_accessed=moved, transcendentals=work
        ),
    )(*args)


def together(values):
    return lax.optimization_barrier(values)


def f32(*shape):
    return jax.ShapeDtypeStruct(shape, jnp.float32)


def bf16(*shape):
    return jax.ShapeDtypeStruct(shape, jnp.bfloat16)


def body(feat_one, feat_two, value_one, value_two):
    total = feat_one.shape[0] * lax.axis_size("row") * lax.axis_size("col")
    scale = math.log2(math.e) / math.sqrt(WIDTH)
    own, feats = call(
        pack_kernel,
        [bf16(2, 2, SHARD, WIDTH), bf16(2, SHARD, WIDTH)],
        (feat_one, value_one, feat_two, value_two),
        scratch=[
            pltpu.VMEM((2, SHARD, WIDTH), jnp.bfloat16),
            pltpu.SemaphoreType.DMA((4,)),
        ],
        specs=[HBM] * 4,
        vmem=62 << 20,
    )

    pieces = [own] + [fast_shift("row", own, -step) for step in range(1, SUB)]
    partner = fast_swap("col", feats, 2)
    sends = [
        jnp.concatenate([piece[side] for piece in pieces] + [partner[side : side + 1]])
        for side in range(2)
    ]
    sends = together(sends)
    tiles = [
        [send] + [slow_shift(axis, send, -step) for step in range(1, SUB)]
        for axis, send in zip(("col", "row"), sends)
    ]
    tiles = together(tiles)
    queries = jnp.stack(
        [tile[index] for side in tiles for tile in side for index in (0, 2 * SUB)]
    )
    others = fast_swap("col", queries, 1)

    def score(side, queries):
        shapes = [f32(2, ROWS, BLOCK)]
        kernel = functools.partial(score_kernel, total, scale, side, side * 2 * SUB)
        work = 2 * SUB * SHARD * SUB * BLOCK
        return call(kernel, shapes, (queries, *tiles[1 - side]), work=work)[0]

    def core_merge(mine, theirs):
        return call(core_kernel, [f32(ROWS, 2 * SHARD)] * SUB, (mine, theirs))

    def spread(axis, parts):
        return [parts[0]] + [slow_shift(axis, parts[step], step) for step in range(1, SUB)]

    keep_one = score(0, queries)
    others, keep_one = together((others, keep_one))
    send_one = score(0, others)
    theirs_one = fast_swap("col", send_one, 1)
    others, _ = together((others, send_one))
    send_two = score(1, others)
    theirs_two = fast_swap("col", send_two, 1)
    rows = core_merge(keep_one, theirs_one)
    queries, _, rows = together((queries, send_two, rows))
    rows = spread("col", rows)
    keep_two = score(1, queries)
    rows, keep_two = together((rows, keep_two))
    cols = spread("row", core_merge(keep_two, theirs_two))
    keep, send = call(chip_kernel, [f32(2, ROWS, SHARD)] * 2, (*rows, *cols))
    theirs = fast_swap("col", send, 2)
    outs = [f32(SHARD, WIDTH), f32(2, SHARD)] * 2
    return tuple(call(functools.partial(finish_kernel, total), outs, (keep, theirs)))


def solution(mesh):
    return jax.shard_map(
        body,
        mesh=mesh,
        in_specs=(
            P(("row", "col"), None),
            P(("col", "row"), None),
            P(("row", "col"), None),
            P(("col", "row"), None),
        ),
        out_specs=(
            P(("row", "col"), None),
            P(None, ("row", "col")),
            P(("col", "row"), None),
            P(None, ("col", "row")),
        ),
        check_vma=False,
    )
```

```python
import functools
import math

import jax
import jax.numpy as jnp
from jax import lax
from jax.experimental import pallas as pl
from jax.experimental.pallas import tpu as pltpu
from jax.sharding import PartitionSpec as P

GRID_W = 256
SUB = 4
SHARD = 128
WIDTH = 128
BLOCK = SUB * SHARD
ROWS = WIDTH + 8
AUG = 16
TOTAL_ROW, ACROSS_ROW, DOWN_ROW, PEAK_ROW = 0, 1, 2, 3
VMEM = pl.BlockSpec(memory_space=pltpu.VMEM)
HBM = pl.BlockSpec(memory_space=pltpu.HBM)


def slow_shift(axis, value, step):
    pairs = [(i, ((i // SUB + step) % SUB) * SUB + i % SUB) for i in range(SUB * SUB)]
    return lax.ppermute(value, axis, pairs)


def fast_shift(axis, value, step):
    pairs = [(i, (i // SUB) * SUB + (i % SUB + step) % SUB) for i in range(SUB * SUB)]
    return lax.ppermute(value, axis, pairs)


def fast_swap(axis, value, step):
    return lax.ppermute(value, axis, [(i, i ^ step) for i in range(SUB * SUB)])


def pack_kernel(feat_one, value_one, feat_two, value_two, both, feats, held, sems):
    copies = []
    for side, value in enumerate((value_one, value_two)):
        copies.append(pltpu.make_async_copy(value, held.at[side], sems.at[side]))
    for side, feat in enumerate((feat_one, feat_two)):
        copies.append(pltpu.make_async_copy(feat, feats.at[side], sems.at[2 + side]))
    for copy in copies:
        copy.start()
    for side in range(2):
        copies[side].wait()
        both[side, 1] = held[side].astype(jnp.float32).T.astype(jnp.bfloat16)
    for side in range(2):
        copies[2 + side].wait()
        both[side, 0] = feats[side]


def piece_coords(start, total):
    across = (start % GRID_W).astype(jnp.float32) / GRID_W
    down = (start // GRID_W).astype(jnp.float32) / (total // GRID_W)
    return across, down


def coord_rows(start, total):
    across, down = piece_coords(start, total)
    sub = lax.broadcasted_iota(jnp.int32, (AUG, SHARD), 0)
    lane = lax.broadcasted_iota(jnp.int32, (AUG, SHARD), 1).astype(jnp.float32) / GRID_W
    rows = jnp.where(sub == DOWN_ROW, down, 0.0)
    rows = jnp.where(sub == ACROSS_ROW, across + lane, rows)
    rows = jnp.where(sub == TOTAL_ROW, 1.0, rows)
    return rows.astype(jnp.bfloat16)


def key_start(side, slow, fast):
    row, col = lax.axis_index("row"), lax.axis_index("col")
    z = (row % SUB + fast) % SUB
    if side == 0:
        y = (row // SUB + slow) % SUB
        return ((col * SUB + y) * SUB + z) * SHARD
    x = (col // SUB + slow) % SUB
    return (((row // SUB * SUB + z) * SUB + x) * SUB + col % SUB) * SHARD


def own_start(side):
    row, col = lax.axis_index("row"), lax.axis_index("col")
    return (row * SUB * SUB + col if side == 0 else col * SUB * SUB + row) * SHARD


def merge(peaks, parts):
    top = peaks[0]
    for peak in peaks[1:]:
        top = jnp.maximum(top, peak)
    whole = None
    for peak, part in zip(peaks, parts):
        term = part * jnp.exp2(peak - top)
        whole = term if whole is None else whole + term
    return top, whole


def with_peak(top, whole):
    sub = lax.broadcasted_iota(jnp.int32, (ROWS - WIDTH, top.shape[1]), 0)
    return jnp.concatenate(
        [whole[:WIDTH], jnp.where(sub == PEAK_ROW, top, whole[WIDTH:])], axis=0
    )


def peak_of(part):
    return part[WIDTH + PEAK_ROW : WIDTH + PEAK_ROW + 1, :]


def merged(parts):
    return with_peak(*merge([peak_of(part) for part in parts], parts))


def attend(scale, query, blocks, carry):
    peaks, parts = [peak_of(part) for part in carry], list(carry)
    for keys, values in blocks:
        score = lax.dot_general(
            keys, query, (((1,), (1,)), ((), ())), preferred_element_type=jnp.float32
        ) * scale
        peak = jnp.max(score, axis=0, keepdims=True)
        weight = jnp.exp2(score - peak).astype(jnp.bfloat16)
        parts.append(jnp.dot(values, weight, preferred_element_type=jnp.float32)[:ROWS])
        peaks.append(peak)
    return with_peak(*merge(peaks, parts))


def score_kernel(total, scale, side, fasts, carried, queries, *refs):
    keys, refs = refs[:SUB], refs[SUB:]
    out = refs[-1]

    def block_of(index, fast):
        feats = jnp.concatenate([key[2 * index] for key in keys], axis=0)
        values = jnp.concatenate([key[2 * index + 1] for key in keys], axis=1)
        extra = [coord_rows(key_start(side, slow, fast), total) for slow in range(SUB)]
        return feats, jnp.concatenate([values, jnp.concatenate(extra, axis=1)], axis=0)

    def step(part, _):
        tiles = [
            queries[(half * 2 + side) * SUB + part * 2 + slow]
            for slow in range(2)
            for half in range(2)
        ]
        query = jnp.concatenate(tiles, axis=0)
        blocks = [block_of(index, fast) for index, fast in enumerate(fasts)]
        carry = [refs[0][part]] if carried else []
        out[part] = attend(scale, query, blocks, carry)
        return 0

    lax.fori_loop(0, 2, step, 0)


def core_kernel(mine, theirs, *outs):
    for part in range(2):
        whole = merged([mine[part], theirs[part]])
        outs[2 * part][...] = whole[:, : 2 * SHARD]
        outs[2 * part + 1][...] = whole[:, 2 * SHARD :]


def chip_kernel(*refs):
    ins, (keep, send) = refs[: 2 * SUB], refs[2 * SUB :]
    for side in range(2):
        whole = merged([ref[...] for ref in ins[side * SUB : (side + 1) * SUB]])
        keep[side] = whole[:, :SHARD]
        send[side] = whole[:, SHARD:]


def finish_kernel(total, mine, theirs, *outs):
    lane = lax.broadcasted_iota(jnp.int32, (1, SHARD), 1).astype(jnp.float32) / GRID_W
    for side in range(2):
        matched, flow = outs[2 * side], outs[2 * side + 1]
        own_across, own_down = piece_coords(own_start(side), total)
        parts = [mine[side], theirs[side]]
        _, whole = merge([peak_of(part) for part in parts], parts)
        inverse = 1.0 / whole[WIDTH + TOTAL_ROW : WIDTH + TOTAL_ROW + 1, :]
        matched[...] = (whole[:WIDTH] * inverse).T
        across = whole[WIDTH + ACROSS_ROW : WIDTH + ACROSS_ROW + 1, :] * inverse
        down = whole[WIDTH + DOWN_ROW : WIDTH + DOWN_ROW + 1, :] * inverse
        flow[0:1, :] = across - (own_across + lane)
        flow[1:2, :] = down - own_down


def call(kernel, shapes, args, scratch=(), work=0, specs=None, vmem=48 << 20):
    moved = sum(math.prod(a.shape) * a.dtype.itemsize for a in (*args, *shapes))
    return pl.pallas_call(
        kernel,
        out_shape=shapes,
        in_specs=specs or [VMEM] * len(args),
        out_specs=[VMEM] * len(shapes),
        scratch_shapes=list(scratch),
        compiler_params=pltpu.CompilerParams(vmem_limit_bytes=vmem),
        cost_estimate=pl.CostEstimate(
            flops=4 * WIDTH * work, bytes_accessed=moved, transcendentals=work
        ),
    )(*args)


def together(values):
    return lax.optimization_barrier(values)


def f32(*shape):
    return jax.ShapeDtypeStruct(shape, jnp.float32)


def bf16(*shape):
    return jax.ShapeDtypeStruct(shape, jnp.bfloat16)


def body(feat_one, feat_two, value_one, value_two):
    total = feat_one.shape[0] * lax.axis_size("row") * lax.axis_size("col")
    scale = math.log2(math.e) / math.sqrt(WIDTH)
    both, feats = call(
        pack_kernel,
        [bf16(2, 2, SHARD, WIDTH), bf16(2, SHARD, WIDTH)],
        (feat_one, value_one, feat_two, value_two),
        scratch=[
            pltpu.VMEM((2, SHARD, WIDTH), jnp.bfloat16),
            pltpu.SemaphoreType.DMA((4,)),
        ],
        specs=[HBM] * 4,
        vmem=62 << 20,
    )

    def gathered(axis, value):
        return [value] + [slow_shift(axis, value, -step) for step in range(1, SUB)]

    partner = fast_swap("col", feats, 2)
    others = [fast_shift("row", both, -step) for step in range(1, SUB)]
    own = [jnp.concatenate([both[side], partner[side : side + 1]]) for side in range(2)]
    near = [gathered("col", own[0]), gathered("row", own[1])]
    sends = [jnp.concatenate([piece[side] for piece in others]) for side in range(2)]
    near, sends = together((near, sends))
    far = [gathered("col", sends[0]), gathered("row", sends[1])]
    queries = jnp.stack([tile[at] for at in (0, 2) for side in near for tile in side])
    partners = fast_swap("col", queries, 1)

    def score(side, queries, keys, fasts, carry=()):
        kernel = functools.partial(score_kernel, total, scale, side, fasts, len(carry))
        work = 2 * SUB * SHARD * SUB * SHARD * len(fasts)
        args = (queries, *keys[1 - side], *carry)
        return call(kernel, [f32(2, ROWS, BLOCK)], args, work=work)[0]

    rest = tuple(range(1, SUB))
    early = [score(side, queries, near, (0,)) for side in range(2)]
    partners, early = together((partners, early))
    early_send = [score(side, partners, near, (0,)) for side in range(2)]
    far[1], early_send = together((far[1], early_send))

    def core_merge(mine, theirs):
        return call(core_kernel, [f32(ROWS, 2 * SHARD)] * SUB, (mine, theirs))

    def spread(axis, parts):
        return [parts[0]] + [slow_shift(axis, parts[step], step) for step in range(1, SUB)]

    send_one = score(0, partners, far, rest, (early_send[0],))
    theirs_one = fast_swap("col", send_one, 1)
    queries, _ = together((queries, send_one))
    keep_one = score(0, queries, far, rest, (early[0],))
    partners, keep_one = together((partners, keep_one))
    send_two = score(1, partners, far, rest, (early_send[1],))
    theirs_two = fast_swap("col", send_two, 1)
    rows = core_merge(keep_one, theirs_one)
    queries, _, rows = together((queries, send_two, rows))
    rows = spread("col", rows)
    keep_two = score(1, queries, far, rest, (early[1],))
    rows, keep_two = together((rows, keep_two))
    cols = spread("row", core_merge(keep_two, theirs_two))
    keep, send = call(chip_kernel, [f32(2, ROWS, SHARD)] * 2, (*rows, *cols))
    theirs = fast_swap("col", send, 2)
    outs = [f32(SHARD, WIDTH), f32(2, SHARD)] * 2
    return tuple(call(functools.partial(finish_kernel, total), outs, (keep, theirs)))


def solution(mesh):
    return jax.shard_map(
        body,
        mesh=mesh,
        in_specs=(
            P(("row", "col"), None),
            P(("col", "row"), None),
            P(("row", "col"), None),
            P(("col", "row"), None),
        ),
        out_specs=(
            P(("row", "col"), None),
            P(None, ("row", "col")),
            P(("col", "row"), None),
            P(None, ("col", "row")),
        ),
        check_vma=False,
    )
```

```python
import functools
import math

import jax
import jax.numpy as jnp
from jax import lax
from jax.experimental import pallas as pl
from jax.experimental.pallas import tpu as pltpu
from jax.sharding import PartitionSpec as P

GRID_W = 256
SUB = 4
SHARD = 128
WIDTH = 128
BLOCK = SUB * SHARD
ROWS = WIDTH + 8
AUG = 16
TOTAL_ROW, ACROSS_ROW, DOWN_ROW, PEAK_ROW = 0, 1, 2, 3
VMEM = pl.BlockSpec(memory_space=pltpu.VMEM)
HBM = pl.BlockSpec(memory_space=pltpu.HBM)


def slow_shift(axis, value, step):
    pairs = [(i, ((i // SUB + step) % SUB) * SUB + i % SUB) for i in range(SUB * SUB)]
    return lax.ppermute(value, axis, pairs)


def fast_shift(axis, value, step):
    pairs = [(i, (i // SUB) * SUB + (i % SUB + step) % SUB) for i in range(SUB * SUB)]
    return lax.ppermute(value, axis, pairs)


def fast_swap(axis, value, step):
    return lax.ppermute(value, axis, [(i, i ^ step) for i in range(SUB * SUB)])


def pack_kernel(feat_one, value_one, feat_two, value_two, out, feats, held, sems):
    sources = ((feat_one, value_one), (feat_two, value_two))
    copies = []
    for side, (feat, value) in enumerate(sources):
        copies.append(pltpu.make_async_copy(value, held.at[side], sems.at[2 * side]))
        copies.append(pltpu.make_async_copy(feat, feats.at[side], sems.at[2 * side + 1]))
    for copy in copies:
        copy.start()
    for side in range(2):
        copies[2 * side].wait()
        out[side, 1] = held[side].astype(jnp.float32).T.astype(jnp.bfloat16)
        copies[2 * side + 1].wait()
        out[side, 0] = feats[side]


def piece_coords(start, total):
    across = (start % GRID_W).astype(jnp.float32) / GRID_W
    down = (start // GRID_W).astype(jnp.float32) / (total // GRID_W)
    return across, down


def coord_rows(start, total):
    across, down = piece_coords(start, total)
    sub = lax.broadcasted_iota(jnp.int32, (AUG, SHARD), 0)
    lane = lax.broadcasted_iota(jnp.int32, (AUG, SHARD), 1).astype(jnp.float32) / GRID_W
    rows = jnp.where(sub == DOWN_ROW, down, 0.0)
    rows = jnp.where(sub == ACROSS_ROW, across + lane, rows)
    rows = jnp.where(sub == TOTAL_ROW, 1.0, rows)
    return rows.astype(jnp.bfloat16)


def key_start(side, slow, fast):
    row, col = lax.axis_index("row"), lax.axis_index("col")
    z = (row % SUB + fast) % SUB
    if side == 0:
        y = (row // SUB + slow) % SUB
        return ((col * SUB + y) * SUB + z) * SHARD
    x = (col // SUB + slow) % SUB
    return (((row // SUB * SUB + z) * SUB + x) * SUB + col % SUB) * SHARD


def own_start(side):
    row, col = lax.axis_index("row"), lax.axis_index("col")
    return (row * SUB * SUB + col if side == 0 else col * SUB * SUB + row) * SHARD


def merge(peaks, parts):
    top = peaks[0]
    for peak in peaks[1:]:
        top = jnp.maximum(top, peak)
    whole = None
    for peak, part in zip(peaks, parts):
        term = part * jnp.exp2(peak - top)
        whole = term if whole is None else whole + term
    return top, whole


def with_peak(top, whole):
    sub = lax.broadcasted_iota(jnp.int32, (ROWS - WIDTH, top.shape[1]), 0)
    return jnp.concatenate(
        [whole[:WIDTH], jnp.where(sub == PEAK_ROW, top, whole[WIDTH:])], axis=0
    )


def peak_of(part):
    return part[WIDTH + PEAK_ROW : WIDTH + PEAK_ROW + 1, :]


def merged(parts):
    return with_peak(*merge([peak_of(part) for part in parts], parts))


def attend(scale, queries, blocks):
    steps = [(tile, block) for tile in range(len(queries)) for block in range(len(blocks))]

    def raw(tile, block):
        return lax.dot_general(
            blocks[block][0],
            queries[tile],
            (((1,), (1,)), ((), ())),
            preferred_element_type=jnp.float32,
        )

    peaks, parts = [[] for _ in queries], [[] for _ in queries]
    ahead = raw(*steps[0])
    for at, (tile, block) in enumerate(steps):
        score = ahead * scale
        if at + 1 < len(steps):
            ahead = raw(*steps[at + 1])
        peak = jnp.max(score, axis=0, keepdims=True)
        weight = jnp.exp2(score - peak).astype(jnp.bfloat16)
        part = jnp.dot(blocks[block][1], weight, preferred_element_type=jnp.float32)
        parts[tile].append(part[:ROWS])
        peaks[tile].append(peak)
    return [with_peak(*merge(*pair)) for pair in zip(peaks, parts)]


def score_kernel(total, scale, side, halves, queries, *refs):
    keys, outs = refs[:SUB], refs[SUB:]

    def block_of(slow):
        tiles = keys[slow]
        feats = jnp.concatenate([tiles[2 * fast] for fast in range(SUB)], axis=0)
        values = jnp.concatenate([tiles[2 * fast + 1] for fast in range(SUB)], axis=1)
        extra = [coord_rows(key_start(side, slow, fast), total) for fast in range(SUB)]
        return feats, jnp.concatenate([values, jnp.concatenate(extra, axis=1)], axis=0)

    blocks = [block_of(slow) for slow in range(SUB)]
    tiles = [
        jnp.concatenate(
            [queries[(side * 2 + half) * SUB + piece] for piece in range(SUB)], axis=0
        )
        for half in halves
    ]
    for index, whole in enumerate(attend(scale, tiles, blocks)):
        outs[0][index] = whole


def core_kernel(halves, *refs):
    (theirs, *mine), outs = refs[: -2 * len(halves)], refs[-2 * len(halves) :]
    for index, half in enumerate(halves):
        own = mine[0][index]
        whole = merged([own, theirs[half]])
        outs[2 * index][...] = whole[:, : 2 * SHARD]
        outs[2 * index + 1][...] = whole[:, 2 * SHARD :]


def chip_kernel(*refs):
    ins, (keep, send) = refs[: 2 * SUB], refs[2 * SUB :]
    for side in range(2):
        whole = merged([ref[...] for ref in ins[side * SUB : (side + 1) * SUB]])
        keep[side] = whole[:, :SHARD]
        send[side] = whole[:, SHARD:]


def finish_kernel(total, mine, theirs, *outs):
    lane = lax.broadcasted_iota(jnp.int32, (1, SHARD), 1).astype(jnp.float32) / GRID_W
    for side in range(2):
        matched, flow = outs[2 * side], outs[2 * side + 1]
        own_across, own_down = piece_coords(own_start(side), total)
        parts = [mine[side], theirs[side]]
        _, whole = merge([peak_of(part) for part in parts], parts)
        inverse = 1.0 / whole[WIDTH + TOTAL_ROW : WIDTH + TOTAL_ROW + 1, :]
        matched[...] = (whole[:WIDTH] * inverse).T
        across = whole[WIDTH + ACROSS_ROW : WIDTH + ACROSS_ROW + 1, :] * inverse
        down = whole[WIDTH + DOWN_ROW : WIDTH + DOWN_ROW + 1, :] * inverse
        flow[0:1, :] = across - (own_across + lane)
        flow[1:2, :] = down - own_down


def call(kernel, shapes, args, scratch=(), work=0, specs=None, vmem=48 << 20):
    moved = sum(math.prod(a.shape) * a.dtype.itemsize for a in (*args, *shapes))
    return pl.pallas_call(
        kernel,
        out_shape=shapes,
        in_specs=specs or [VMEM] * len(args),
        out_specs=[VMEM] * len(shapes),
        scratch_shapes=list(scratch),
        compiler_params=pltpu.CompilerParams(vmem_limit_bytes=vmem),
        cost_estimate=pl.CostEstimate(
            flops=4 * WIDTH * work, bytes_accessed=moved, transcendentals=work
        ),
    )(*args)


def together(values):
    return lax.optimization_barrier(values)


def f32(*shape):
    return jax.ShapeDtypeStruct(shape, jnp.float32)


def bf16(*shape):
    return jax.ShapeDtypeStruct(shape, jnp.bfloat16)


def body(feat_one, feat_two, value_one, value_two):
    total = feat_one.shape[0] * lax.axis_size("row") * lax.axis_size("col")
    scale = math.log2(math.e) / math.sqrt(WIDTH)
    own, feats = call(
        pack_kernel,
        [bf16(2, 2, SHARD, WIDTH), bf16(2, SHARD, WIDTH)],
        (feat_one, value_one, feat_two, value_two),
        scratch=[
            pltpu.VMEM((2, SHARD, WIDTH), jnp.bfloat16),
            pltpu.SemaphoreType.DMA((4,)),
        ],
        specs=[HBM] * 4,
        vmem=62 << 20,
    )

    pieces = [own] + [fast_shift("row", own, -step) for step in range(1, SUB)]
    partner = fast_swap("col", feats, 2)
    sends = [
        jnp.concatenate([piece[side] for piece in pieces] + [partner[side : side + 1]])
        for side in range(2)
    ]
    sends = together(sends)
    tiles = [
        [send] + [slow_shift(axis, send, -step) for step in range(1, SUB)]
        for axis, send in zip(("col", "row"), sends)
    ]
    tiles = together(tiles)
    queries = jnp.stack(
        [tile[index] for side in tiles for tile in side for index in (0, 2 * SUB)]
    )
    others = fast_swap("col", queries, 1)

    def score(side, queries, *halves):
        shapes = [f32(len(halves), ROWS, BLOCK)]
        kernel = functools.partial(score_kernel, total, scale, side, halves)
        work = len(halves) * SUB * SHARD * SUB * BLOCK
        return call(kernel, shapes, (queries, *tiles[1 - side]), work=work)[0]

    def core_merge(mine, theirs, *halves):
        shapes = [f32(ROWS, 2 * SHARD)] * (2 * len(halves))
        return call(functools.partial(core_kernel, halves), shapes, (theirs, mine))

    def spread(axis, parts, first=0):
        return [
            slow_shift(axis, part, first + step) if first + step else part
            for step, part in enumerate(parts)
        ]

    keep_one = score(0, queries, 0, 1)
    others, keep_one = together((others, keep_one))
    send_one = score(0, others, 0, 1)
    theirs_one = fast_swap("col", send_one, 1)
    others, _ = together((others, send_one))
    send_two = score(1, others, 0, 1)
    theirs_two = fast_swap("col", send_two, 1)
    rows = core_merge(keep_one, theirs_one, 0, 1)
    queries, _, rows = together((queries, send_two, rows))
    rows = spread("col", rows)
    far_two = score(1, queries, 1)
    far_cols = core_merge(far_two, theirs_two, 1)
    queries, far_cols = together((queries, far_cols))
    far_cols = spread("row", far_cols, 2)
    near_two = score(1, queries, 0)
    rows, near_two = together((rows, near_two))
    cols = spread("row", core_merge(near_two, theirs_two, 0)) + far_cols
    keep, send = call(chip_kernel, [f32(2, ROWS, SHARD)] * 2, (*rows, *cols))
    theirs = fast_swap("col", send, 2)
    outs = [f32(SHARD, WIDTH), f32(2, SHARD)] * 2
    return tuple(call(functools.partial(finish_kernel, total), outs, (keep, theirs)))


def solution(mesh):
    return jax.shard_map(
        body,
        mesh=mesh,
        in_specs=(
            P(("row", "col"), None),
            P(("col", "row"), None),
            P(("row", "col"), None),
            P(("col", "row"), None),
        ),
        out_specs=(
            P(("row", "col"), None),
            P(None, ("row", "col")),
            P(("col", "row"), None),
            P(None, ("col", "row")),
        ),
        check_vma=False,
    )
```

```python
import functools
import math

import jax
import jax.numpy as jnp
from jax import lax
from jax.experimental import pallas as pl
from jax.experimental.pallas import tpu as pltpu
from jax.sharding import PartitionSpec as P

GRID_W = 256
SUB = 4
SHARD = 128
WIDTH = 128
BLOCK = SUB * SHARD
ROWS = WIDTH + 8
AUG = 16
TOTAL_ROW, ACROSS_ROW, DOWN_ROW, PEAK_ROW = 0, 1, 2, 3
VMEM = pl.BlockSpec(memory_space=pltpu.VMEM)
HBM = pl.BlockSpec(memory_space=pltpu.HBM)


def slow_shift(axis, value, step):
    pairs = [(i, ((i // SUB + step) % SUB) * SUB + i % SUB) for i in range(SUB * SUB)]
    return lax.ppermute(value, axis, pairs)


def fast_shift(axis, value, step):
    pairs = [(i, (i // SUB) * SUB + (i % SUB + step) % SUB) for i in range(SUB * SUB)]
    return lax.ppermute(value, axis, pairs)


def fast_swap(axis, value, step):
    return lax.ppermute(value, axis, [(i, i ^ step) for i in range(SUB * SUB)])


def pack_kernel(feat_one, value_one, feat_two, value_two, out_one, out_two, held, sems):
    copies = [
        pltpu.make_async_copy(feat_one, out_one.at[:, :WIDTH], sems.at[0]),
        pltpu.make_async_copy(feat_two, out_two.at[:, :WIDTH], sems.at[1]),
        pltpu.make_async_copy(value_one, held.at[0], sems.at[2]),
        pltpu.make_async_copy(value_two, held.at[1], sems.at[3]),
    ]
    for copy in copies:
        copy.start()
    for side, out in ((0, out_one), (1, out_two)):
        copies[2 + side].wait()
        out[:, WIDTH:] = held[side].astype(jnp.float32).T.astype(jnp.bfloat16)
    copies[0].wait()
    copies[1].wait()


def piece_coords(start, total):
    across = (start % GRID_W).astype(jnp.float32) / GRID_W
    down = (start // GRID_W).astype(jnp.float32) / (total // GRID_W)
    return across, down


def coord_rows(start, total):
    across, down = piece_coords(start, total)
    sub = lax.broadcasted_iota(jnp.int32, (AUG, SHARD), 0)
    lane = lax.broadcasted_iota(jnp.int32, (AUG, SHARD), 1).astype(jnp.float32) / GRID_W
    rows = jnp.where(sub == DOWN_ROW, down, 0.0)
    rows = jnp.where(sub == ACROSS_ROW, across + lane, rows)
    rows = jnp.where(sub == TOTAL_ROW, 1.0, rows)
    return rows.astype(jnp.bfloat16)


def block_of(pieces, starts, total):
    keys = jnp.concatenate([piece[:, :WIDTH] for piece in pieces], axis=0)
    values = jnp.concatenate([piece[:, WIDTH:] for piece in pieces], axis=1)
    extra = jnp.concatenate([coord_rows(start, total) for start in starts], axis=1)
    return keys, jnp.concatenate([values, extra], axis=0)


def start_one(slow, fast_high, fast_low):
    row, col = lax.axis_index("row"), lax.axis_index("col")
    x = (col // SUB + slow) % SUB
    fast = (col % SUB) ^ (2 * fast_high + fast_low)
    return ((row * SUB + x) * SUB + fast) * SHARD


def start_two(slow, fast):
    row, col = lax.axis_index("row"), lax.axis_index("col")
    y = (row // SUB + slow) % SUB
    z = (row % SUB + fast) % SUB
    return ((col * SUB + y) * SUB + z) * SHARD


def merge(peaks, parts):
    top = peaks[0]
    for peak in peaks[1:]:
        top = jnp.maximum(top, peak)
    whole = None
    for peak, part in zip(peaks, parts):
        term = part * jnp.exp2(peak - top)
        whole = term if whole is None else whole + term
    return top, whole


def with_peak(top, whole):
    sub = lax.broadcasted_iota(jnp.int32, (ROWS - WIDTH, top.shape[1]), 0)
    return jnp.concatenate(
        [whole[:WIDTH], jnp.where(sub == PEAK_ROW, top, whole[WIDTH:])], axis=0
    )


def peak_of(part):
    return part[WIDTH + PEAK_ROW : WIDTH + PEAK_ROW + 1, :]


def merged(parts):
    return with_peak(*merge([peak_of(part) for part in parts], parts))


def attend(scale, queries, blocks):
    steps = [(tile, block) for tile in range(len(queries)) for block in range(len(blocks))]

    def raw(tile, block):
        return lax.dot_general(
            blocks[block][0],
            queries[tile],
            (((1,), (1,)), ((), ())),
            preferred_element_type=jnp.float32,
        )

    peaks, parts = [[] for _ in queries], [[] for _ in queries]
    ahead = raw(*steps[0])
    for at, (tile, block) in enumerate(steps):
        score = ahead * scale
        if at + 1 < len(steps):
            ahead = raw(*steps[at + 1])
        peak = jnp.max(score, axis=0, keepdims=True)
        weight = jnp.exp2(score - peak).astype(jnp.bfloat16)
        part = jnp.dot(blocks[block][1], weight, preferred_element_type=jnp.float32)
        parts[tile].append(part[:ROWS])
        peaks[tile].append(peak)
    return [with_peak(*merge(*pair)) for pair in zip(peaks, parts)]


def one_block(ones, slow, total):
    pieces = [ones[low * 2 + high][slow] for low in range(2) for high in range(2)]
    starts = [start_one(slow, high, low) for low in range(2) for high in range(2)]
    return block_of(pieces, starts, total)


def two_block(two, slow, total):
    return block_of(
        [two[piece] for piece in range(SUB)],
        [start_two(slow, piece) for piece in range(SUB)],
        total,
    )


def col_kernel(total, scale, *refs):
    ones, two, out = refs[:SUB], refs[SUB], refs[SUB + 1]
    query = jnp.concatenate([two[piece, :, :WIDTH] for piece in range(SUB)], axis=0)
    blocks = [one_block(ones, slow, total) for slow in range(SUB)]
    (out[...],) = attend(scale, [query], blocks)


def row_kernel(total, scale, halves, *refs):
    ones, twos, outs = refs[:SUB], refs[SUB : 2 * SUB], refs[2 * SUB :]
    tiles = [
        jnp.concatenate(
            [
                ones[2 * core + high][slow, :, :WIDTH]
                for slow in (2 * half, 2 * half + 1)
                for high in range(2)
            ],
            axis=0,
        )
        for core, half in halves
    ]
    blocks = [two_block(two, block, total) for block, two in enumerate(twos)]
    wholes = attend(scale, tiles, blocks)
    for out in outs:
        for index in range(out.shape[0]):
            out[index] = wholes.pop(0)


def core_kernel(halves, *refs):
    (theirs, *mine), outs = refs[: -2 * len(halves)], refs[-2 * len(halves) :]
    for index, half in enumerate(halves):
        own = mine[0][index]
        whole = merged([own, theirs[half]])
        outs[2 * index][...] = whole[:, : 2 * SHARD]
        outs[2 * index + 1][...] = whole[:, 2 * SHARD :]


def chip_kernel(*refs):
    ins, (keep, send) = refs[:SUB], refs[SUB:]
    whole = merged([ref[...] for ref in ins])
    keep[...] = whole[:, :SHARD]
    send[...] = whole[:, SHARD:]


def block_kernel(*refs):
    ins, outs = refs[:SUB], refs[SUB:]
    for piece in range(SUB):
        span = slice(piece * SHARD, (piece + 1) * SHARD)
        outs[piece][...] = merged([ref[:, span] for ref in ins])


def finish_kernel(total, own_start, *refs):
    ins, (matched, flow) = refs[:-2], refs[-2:]
    own_across, own_down = piece_coords(own_start(), total)
    lane = lax.broadcasted_iota(jnp.int32, (1, SHARD), 1).astype(jnp.float32) / GRID_W
    parts = [ref[...] for ref in ins]
    _, whole = merge([peak_of(part) for part in parts], parts)
    inverse = 1.0 / whole[WIDTH + TOTAL_ROW : WIDTH + TOTAL_ROW + 1, :]
    matched[...] = (whole[:WIDTH] * inverse).T
    across = whole[WIDTH + ACROSS_ROW : WIDTH + ACROSS_ROW + 1, :] * inverse
    down = whole[WIDTH + DOWN_ROW : WIDTH + DOWN_ROW + 1, :] * inverse
    flow[0:1, :] = across - (own_across + lane)
    flow[1:2, :] = down - own_down


def call(kernel, shapes, args, scratch=(), work=0, specs=None, vmem=48 << 20):
    moved = sum(math.prod(a.shape) * a.dtype.itemsize for a in (*args, *shapes))
    return pl.pallas_call(
        kernel,
        out_shape=shapes,
        in_specs=specs or [VMEM] * len(args),
        out_specs=[VMEM] * len(shapes),
        scratch_shapes=list(scratch),
        compiler_params=pltpu.CompilerParams(vmem_limit_bytes=vmem),
        cost_estimate=pl.CostEstimate(
            flops=4 * WIDTH * work, bytes_accessed=moved, transcendentals=work
        ),
    )(*args)


def together(values):
    return lax.optimization_barrier(values)


def f32(*shape):
    return jax.ShapeDtypeStruct(shape, jnp.float32)


def bf16(*shape):
    return jax.ShapeDtypeStruct(shape, jnp.bfloat16)


def body(feat_one, feat_two, value_one, value_two):
    total = feat_one.shape[0] * lax.axis_size("row") * lax.axis_size("col")
    scale = math.log2(math.e) / math.sqrt(WIDTH)
    packed = jax.ShapeDtypeStruct((SHARD, 2 * WIDTH), jnp.bfloat16)
    own_one, own_two = call(
        pack_kernel,
        [packed] * 2,
        (feat_one, value_one, feat_two, value_two),
        scratch=[
            pltpu.VMEM((2, SHARD, WIDTH), jnp.bfloat16),
            pltpu.SemaphoreType.DMA((4,)),
        ],
        specs=[HBM] * 4,
        vmem=62 << 20,
    )

    two = [own_two] + [fast_shift("row", own_two, -step) for step in range(1, SUB)]
    one = [own_one, fast_swap("col", own_one, 2)]
    one, two = together((jnp.stack(one), jnp.stack(two)))
    one = [one] + [slow_shift("col", one, -step) for step in range(1, SUB)]
    near, far = slow_shift("row", two, -1), slow_shift("row", two, 1)
    one, near, far = together((jnp.stack(one, axis=1), near, far))
    twos = [two, near, slow_shift("row", two, -2), far]
    other = fast_swap("col", one, 1)
    ones = [one[0], one[1], other[0], other[1]]

    def col_scores(*refs):
        col_kernel(total, scale, *refs)

    def row_scores(ones, halves, weight, *counts):
        shapes = [f32(count, ROWS, BLOCK) for count in counts]
        kernel = functools.partial(row_kernel, total, scale, halves)
        return call(kernel, shapes, (*ones, *twos), work=weight * work)

    def core_merge(mine, theirs, *halves):
        shapes = [f32(ROWS, 2 * SHARD)] * (2 * len(halves))
        return call(functools.partial(core_kernel, halves), shapes, (theirs, mine))

    def spread(axis, parts, first=0):
        return [
            slow_shift(axis, part, first + step) if first + step else part
            for step, part in enumerate(parts)
        ]

    def finish_one(*refs):
        finish_kernel(total, lambda: start_one(0, 0, 0), *refs)

    def finish_two(*refs):
        finish_kernel(total, lambda: start_two(0, 0), *refs)

    work = BLOCK * BLOCK * SUB
    cols = [None] * SUB
    for step in (0, 1, 3, 2):
        if step == 2:
            twos[2], _ = together((twos[2], cols[0]))
        (cols[step],) = call(col_scores, [f32(ROWS, BLOCK)], (*ones, twos[step]), work=work)
    ones, cols = together((ones, cols))
    cols = spread("row", cols)
    send_one, far_one = row_scores(ones, ((1, 0), (1, 1), (0, 1)), 3, 2, 1)
    theirs_one = fast_swap("col", send_one, 1)
    far_rows = core_merge(far_one, theirs_one, 1)
    far_rows = spread("col", far_rows, 2)
    cols = call(block_kernel, [f32(ROWS, SHARD)] * SUB, cols)
    ones, _, cols = together((ones, far_one, cols))
    cols = [cols[0]] + [fast_shift("row", cols[step], step) for step in range(1, SUB)]
    (near_one,) = row_scores(ones, ((0, 0),), 40, 1)
    rows = spread("col", core_merge(near_one, theirs_one, 0)) + far_rows
    keep, send = call(chip_kernel, [f32(ROWS, SHARD)] * 2, rows)
    theirs = fast_swap("col", send, 2)
    outs = [f32(SHARD, WIDTH), f32(2, SHARD)]
    matched_two, flow_two = call(finish_two, outs, cols)
    matched_one, flow_one = call(finish_one, outs, (keep, theirs))
    return matched_one, flow_one, matched_two, flow_two


def solution(mesh):
    return jax.shard_map(
        body,
        mesh=mesh,
        in_specs=(
            P(("row", "col"), None),
            P(("col", "row"), None),
            P(("row", "col"), None),
            P(("col", "row"), None),
        ),
        out_specs=(
            P(("row", "col"), None),
            P(None, ("row", "col")),
            P(("col", "row"), None),
            P(None, ("col", "row")),
        ),
        check_vma=False,
    )
```

```python
import functools
import math

import jax
import jax.numpy as jnp
from jax import lax
from jax.experimental import pallas as pl
from jax.experimental.pallas import tpu as pltpu
from jax.sharding import PartitionSpec as P

GRID_W = 256
SUB = 4
SHARD = 128
WIDTH = 128
BLOCK = SUB * SHARD
ROWS = WIDTH + 8
AUG = 16
TOTAL_ROW, ACROSS_ROW, DOWN_ROW, PEAK_ROW = 0, 1, 2, 3
VMEM = pl.BlockSpec(memory_space=pltpu.VMEM)
HBM = pl.BlockSpec(memory_space=pltpu.HBM)


def slow_shift(axis, value, step):
    pairs = [(i, ((i // SUB + step) % SUB) * SUB + i % SUB) for i in range(SUB * SUB)]
    return lax.ppermute(value, axis, pairs)


def fast_shift(axis, value, step):
    pairs = [(i, (i // SUB) * SUB + (i % SUB + step) % SUB) for i in range(SUB * SUB)]
    return lax.ppermute(value, axis, pairs)


def fast_swap(axis, value, step):
    return lax.ppermute(value, axis, [(i, i ^ step) for i in range(SUB * SUB)])


def pack_kernel(feat_one, value_one, feat_two, value_two, out_one, out_two, held, sems):
    copies = [
        pltpu.make_async_copy(feat_one, out_one.at[:, :WIDTH], sems.at[0]),
        pltpu.make_async_copy(feat_two, out_two.at[:, :WIDTH], sems.at[1]),
        pltpu.make_async_copy(value_one, held.at[0], sems.at[2]),
        pltpu.make_async_copy(value_two, held.at[1], sems.at[3]),
    ]
    for copy in copies:
        copy.start()
    for side, out in ((0, out_one), (1, out_two)):
        copies[2 + side].wait()
        out[:, WIDTH:] = held[side].astype(jnp.float32).T.astype(jnp.bfloat16)
    copies[0].wait()
    copies[1].wait()


def piece_coords(start, total):
    across = (start % GRID_W).astype(jnp.float32) / GRID_W
    down = (start // GRID_W).astype(jnp.float32) / (total // GRID_W)
    return across, down


def coord_rows(start, total):
    across, down = piece_coords(start, total)
    sub = lax.broadcasted_iota(jnp.int32, (AUG, SHARD), 0)
    lane = lax.broadcasted_iota(jnp.int32, (AUG, SHARD), 1).astype(jnp.float32) / GRID_W
    rows = jnp.where(sub == DOWN_ROW, down, 0.0)
    rows = jnp.where(sub == ACROSS_ROW, across + lane, rows)
    rows = jnp.where(sub == TOTAL_ROW, 1.0, rows)
    return rows.astype(jnp.bfloat16)


def block_of(pieces, starts, total):
    keys = jnp.concatenate([piece[:, :WIDTH] for piece in pieces], axis=0)
    values = jnp.concatenate([piece[:, WIDTH:] for piece in pieces], axis=1)
    extra = jnp.concatenate([coord_rows(start, total) for start in starts], axis=1)
    return keys, jnp.concatenate([values, extra], axis=0)


def start_one(slow, fast_high, fast_low):
    row, col = lax.axis_index("row"), lax.axis_index("col")
    x = (col // SUB + slow) % SUB
    fast = (col % SUB) ^ (2 * fast_high + fast_low)
    return ((row * SUB + x) * SUB + fast) * SHARD


def start_two(slow, fast):
    row, col = lax.axis_index("row"), lax.axis_index("col")
    y = (row // SUB + slow) % SUB
    z = (row % SUB + fast) % SUB
    return ((col * SUB + y) * SUB + z) * SHARD


def merge(peaks, parts):
    top = peaks[0]
    for peak in peaks[1:]:
        top = jnp.maximum(top, peak)
    whole = None
    for peak, part in zip(peaks, parts):
        term = part * jnp.exp2(peak - top)
        whole = term if whole is None else whole + term
    return top, whole


def with_peak(top, whole):
    sub = lax.broadcasted_iota(jnp.int32, (ROWS - WIDTH, top.shape[1]), 0)
    return jnp.concatenate(
        [whole[:WIDTH], jnp.where(sub == PEAK_ROW, top, whole[WIDTH:])], axis=0
    )


def peak_of(part):
    return part[WIDTH + PEAK_ROW : WIDTH + PEAK_ROW + 1, :]


def merged(parts):
    return with_peak(*merge([peak_of(part) for part in parts], parts))


def attend(scale, queries, blocks):
    steps = [(tile, block) for tile in range(len(queries)) for block in range(len(blocks))]

    def raw(tile, block):
        return lax.dot_general(
            blocks[block][0],
            queries[tile],
            (((1,), (1,)), ((), ())),
            preferred_element_type=jnp.float32,
        )

    peaks, parts = [[] for _ in queries], [[] for _ in queries]
    ahead = raw(*steps[0])
    for at, (tile, block) in enumerate(steps):
        score = ahead * scale
        if at + 1 < len(steps):
            ahead = raw(*steps[at + 1])
        peak = jnp.max(score, axis=0, keepdims=True)
        weight = jnp.exp2(score - peak).astype(jnp.bfloat16)
        part = jnp.dot(blocks[block][1], weight, preferred_element_type=jnp.float32)
        parts[tile].append(part[:ROWS])
        peaks[tile].append(peak)
    return [with_peak(*merge(*pair)) for pair in zip(peaks, parts)]


def one_block(ones, slow, total):
    pieces = [ones[low * 2 + high][slow] for low in range(2) for high in range(2)]
    starts = [start_one(slow, high, low) for low in range(2) for high in range(2)]
    return block_of(pieces, starts, total)


def two_block(two, slow, total):
    return block_of(
        [two[piece] for piece in range(SUB)],
        [start_two(slow, piece) for piece in range(SUB)],
        total,
    )


def col_kernel(total, scale, *refs):
    ones, two, out = refs[:SUB], refs[SUB], refs[SUB + 1]
    query = jnp.concatenate([two[piece, :, :WIDTH] for piece in range(SUB)], axis=0)
    blocks = [one_block(ones, slow, total) for slow in range(SUB)]
    (out[...],) = attend(scale, [query], blocks)


def row_kernel(total, scale, halves, *refs):
    ones, twos, outs = refs[:SUB], refs[SUB : 2 * SUB], refs[2 * SUB :]
    tiles = [
        jnp.concatenate(
            [
                ones[2 * core + high][slow, :, :WIDTH]
                for slow in (2 * half, 2 * half + 1)
                for high in range(2)
            ],
            axis=0,
        )
        for core, half in halves
    ]
    blocks = [two_block(two, block, total) for block, two in enumerate(twos)]
    wholes = attend(scale, tiles, blocks)
    for out in outs:
        for index in range(out.shape[0]):
            out[index] = wholes.pop(0)


def core_kernel(halves, *refs):
    (theirs, *mine), outs = refs[: -2 * len(halves)], refs[-2 * len(halves) :]
    for index, half in enumerate(halves):
        own = mine[0][index]
        whole = merged([own, theirs[half]])
        outs[2 * index][...] = whole[:, : 2 * SHARD]
        outs[2 * index + 1][...] = whole[:, 2 * SHARD :]


def chip_kernel(*refs):
    ins, (keep, send) = refs[:SUB], refs[SUB:]
    whole = merged([ref[...] for ref in ins])
    keep[...] = whole[:, :SHARD]
    send[...] = whole[:, SHARD:]


def block_kernel(*refs):
    ins, outs = refs[:SUB], refs[SUB:]
    for piece in range(SUB):
        span = slice(piece * SHARD, (piece + 1) * SHARD)
        outs[piece][...] = merged([ref[:, span] for ref in ins])


def finish_kernel(total, own_start, *refs):
    ins, (matched, flow) = refs[:-2], refs[-2:]
    own_across, own_down = piece_coords(own_start(), total)
    lane = lax.broadcasted_iota(jnp.int32, (1, SHARD), 1).astype(jnp.float32) / GRID_W
    parts = [ref[...] for ref in ins]
    _, whole = merge([peak_of(part) for part in parts], parts)
    inverse = 1.0 / whole[WIDTH + TOTAL_ROW : WIDTH + TOTAL_ROW + 1, :]
    matched[...] = (whole[:WIDTH] * inverse).T
    across = whole[WIDTH + ACROSS_ROW : WIDTH + ACROSS_ROW + 1, :] * inverse
    down = whole[WIDTH + DOWN_ROW : WIDTH + DOWN_ROW + 1, :] * inverse
    flow[0:1, :] = across - (own_across + lane)
    flow[1:2, :] = down - own_down


def call(kernel, shapes, args, scratch=(), work=0, specs=None, vmem=48 << 20):
    moved = sum(math.prod(a.shape) * a.dtype.itemsize for a in (*args, *shapes))
    return pl.pallas_call(
        kernel,
        out_shape=shapes,
        in_specs=specs or [VMEM] * len(args),
        out_specs=[VMEM] * len(shapes),
        scratch_shapes=list(scratch),
        compiler_params=pltpu.CompilerParams(vmem_limit_bytes=vmem),
        cost_estimate=pl.CostEstimate(
            flops=4 * WIDTH * work, bytes_accessed=moved, transcendentals=work
        ),
    )(*args)


def together(values):
    return lax.optimization_barrier(values)


def f32(*shape):
    return jax.ShapeDtypeStruct(shape, jnp.float32)


def bf16(*shape):
    return jax.ShapeDtypeStruct(shape, jnp.bfloat16)


def body(feat_one, feat_two, value_one, value_two):
    total = feat_one.shape[0] * lax.axis_size("row") * lax.axis_size("col")
    scale = math.log2(math.e) / math.sqrt(WIDTH)
    packed = jax.ShapeDtypeStruct((SHARD, 2 * WIDTH), jnp.bfloat16)
    own_one, own_two = call(
        pack_kernel,
        [packed] * 2,
        (feat_one, value_one, feat_two, value_two),
        scratch=[
            pltpu.VMEM((2, SHARD, WIDTH), jnp.bfloat16),
            pltpu.SemaphoreType.DMA((4,)),
        ],
        specs=[HBM] * 4,
        vmem=62 << 20,
    )

    two = [own_two] + [fast_shift("row", own_two, -step) for step in range(1, SUB)]
    one = [own_one, fast_swap("col", own_one, 2)]
    one, two = together((jnp.stack(one), jnp.stack(two)))
    one = [one] + [slow_shift("col", one, -step) for step in range(1, SUB)]
    twos = [two] + [slow_shift("row", two, -step) for step in range(1, SUB)]
    one, twos = together((jnp.stack(one, axis=1), twos))
    other = fast_swap("col", one, 1)
    ones = [one[0], one[1], other[0], other[1]]

    def col_scores(*refs):
        col_kernel(total, scale, *refs)

    def row_scores(ones, halves, weight, *counts):
        shapes = [f32(count, ROWS, BLOCK) for count in counts]
        kernel = functools.partial(row_kernel, total, scale, halves)
        return call(kernel, shapes, (*ones, *twos), work=weight * work)

    def core_merge(mine, theirs, *halves):
        shapes = [f32(ROWS, 2 * SHARD)] * (2 * len(halves))
        return call(functools.partial(core_kernel, halves), shapes, (theirs, mine))

    def spread(axis, parts, first=0):
        return [
            slow_shift(axis, part, first + step) if first + step else part
            for step, part in enumerate(parts)
        ]

    def finish_one(*refs):
        finish_kernel(total, lambda: start_one(0, 0, 0), *refs)

    def finish_two(*refs):
        finish_kernel(total, lambda: start_two(0, 0), *refs)

    work = BLOCK * BLOCK * SUB
    cols = [None] * SUB
    for step in (1, 3, 2, 0):
        (cols[step],) = call(col_scores, [f32(ROWS, BLOCK)], (*ones, twos[step]), work=work)
    ones, _ = together((ones, cols))
    cols = spread("row", cols)
    send_one, far_one = row_scores(ones, ((1, 0), (1, 1), (0, 1)), 3, 2, 1)
    theirs_one = fast_swap("col", send_one, 1)
    far_rows = core_merge(far_one, theirs_one, 1)
    far_rows = spread("col", far_rows, 2)
    cols = call(block_kernel, [f32(ROWS, SHARD)] * SUB, cols)
    ones, _, cols = together((ones, far_one, cols))
    cols = [cols[0]] + [fast_shift("row", cols[step], step) for step in range(1, SUB)]
    (near_one,) = row_scores(ones, ((0, 0),), 40, 1)
    rows = spread("col", core_merge(near_one, theirs_one, 0)) + far_rows
    keep, send = call(chip_kernel, [f32(ROWS, SHARD)] * 2, rows)
    theirs = fast_swap("col", send, 2)
    outs = [f32(SHARD, WIDTH), f32(2, SHARD)]
    matched_two, flow_two = call(finish_two, outs, cols)
    matched_one, flow_one = call(finish_one, outs, (keep, theirs))
    return matched_one, flow_one, matched_two, flow_two


def solution(mesh):
    return jax.shard_map(
        body,
        mesh=mesh,
        in_specs=(
            P(("row", "col"), None),
            P(("col", "row"), None),
            P(("row", "col"), None),
            P(("col", "row"), None),
        ),
        out_specs=(
            P(("row", "col"), None),
            P(None, ("row", "col")),
            P(("col", "row"), None),
            P(None, ("col", "row")),
        ),
        check_vma=False,
    )
```

```python
import functools
import math

import jax
import jax.numpy as jnp
from jax import lax
from jax.experimental import pallas as pl
from jax.experimental.pallas import tpu as pltpu
from jax.sharding import PartitionSpec as P

GRID_W = 256
SUB = 4
SHARD = 128
WIDTH = 128
BLOCK = SUB * SHARD
ROWS = WIDTH + 8
AUG = 16
TOTAL_ROW, ACROSS_ROW, DOWN_ROW, PEAK_ROW = 0, 1, 2, 3
VMEM = pl.BlockSpec(memory_space=pltpu.VMEM)
HBM = pl.BlockSpec(memory_space=pltpu.HBM)


def slow_shift(axis, value, step):
    pairs = [(i, ((i // SUB + step) % SUB) * SUB + i % SUB) for i in range(SUB * SUB)]
    return lax.ppermute(value, axis, pairs)


def fast_shift(axis, value, step):
    pairs = [(i, (i // SUB) * SUB + (i % SUB + step) % SUB) for i in range(SUB * SUB)]
    return lax.ppermute(value, axis, pairs)


def fast_swap(axis, value, step):
    return lax.ppermute(value, axis, [(i, i ^ step) for i in range(SUB * SUB)])


def pack_kernel(feat_one, value_one, feat_two, value_two, out_one, out_two, held, sems):
    copies = [
        pltpu.make_async_copy(feat_one, out_one.at[:, :WIDTH], sems.at[0]),
        pltpu.make_async_copy(feat_two, out_two.at[:, :WIDTH], sems.at[1]),
        pltpu.make_async_copy(value_one, held.at[0], sems.at[2]),
        pltpu.make_async_copy(value_two, held.at[1], sems.at[3]),
    ]
    for copy in copies:
        copy.start()
    for side, out in ((0, out_one), (1, out_two)):
        copies[2 + side].wait()
        out[:, WIDTH:] = held[side].astype(jnp.float32).T.astype(jnp.bfloat16)
    copies[0].wait()
    copies[1].wait()


def piece_coords(start, total):
    across = (start % GRID_W).astype(jnp.float32) / GRID_W
    down = (start // GRID_W).astype(jnp.float32) / (total // GRID_W)
    return across, down


def coord_rows(start, total):
    across, down = piece_coords(start, total)
    sub = lax.broadcasted_iota(jnp.int32, (AUG, SHARD), 0)
    lane = lax.broadcasted_iota(jnp.int32, (AUG, SHARD), 1).astype(jnp.float32) / GRID_W
    rows = jnp.where(sub == DOWN_ROW, down, 0.0)
    rows = jnp.where(sub == ACROSS_ROW, across + lane, rows)
    rows = jnp.where(sub == TOTAL_ROW, 1.0, rows)
    return rows.astype(jnp.bfloat16)


def block_of(pieces, starts, total):
    keys = jnp.concatenate([piece[:, :WIDTH] for piece in pieces], axis=0)
    values = jnp.concatenate([piece[:, WIDTH:] for piece in pieces], axis=1)
    extra = jnp.concatenate([coord_rows(start, total) for start in starts], axis=1)
    return keys, jnp.concatenate([values, extra], axis=0)


def start_one(slow, fast_high, fast_low):
    row, col = lax.axis_index("row"), lax.axis_index("col")
    x = (col // SUB + slow) % SUB
    fast = (col % SUB) ^ (2 * fast_high + fast_low)
    return ((row * SUB + x) * SUB + fast) * SHARD


def start_two(slow, fast):
    row, col = lax.axis_index("row"), lax.axis_index("col")
    y = (row // SUB + slow) % SUB
    z = (row % SUB + fast) % SUB
    return ((col * SUB + y) * SUB + z) * SHARD


def merge(peaks, parts):
    top = peaks[0]
    for peak in peaks[1:]:
        top = jnp.maximum(top, peak)
    whole = None
    for peak, part in zip(peaks, parts):
        term = part * jnp.exp2(peak - top)
        whole = term if whole is None else whole + term
    return top, whole


def with_peak(top, whole):
    sub = lax.broadcasted_iota(jnp.int32, (ROWS - WIDTH, top.shape[1]), 0)
    return jnp.concatenate(
        [whole[:WIDTH], jnp.where(sub == PEAK_ROW, top, whole[WIDTH:])], axis=0
    )


def peak_of(part):
    return part[WIDTH + PEAK_ROW : WIDTH + PEAK_ROW + 1, :]


def merged(parts):
    return with_peak(*merge([peak_of(part) for part in parts], parts))


def attend(scale, queries, blocks):
    steps = [(tile, block) for tile in range(len(queries)) for block in range(len(blocks))]

    def raw(tile, block):
        return lax.dot_general(
            blocks[block][0],
            queries[tile],
            (((1,), (1,)), ((), ())),
            preferred_element_type=jnp.float32,
        )

    peaks, parts = [[] for _ in queries], [[] for _ in queries]
    ahead = raw(*steps[0])
    for at, (tile, block) in enumerate(steps):
        score = ahead * scale
        if at + 1 < len(steps):
            ahead = raw(*steps[at + 1])
        peak = jnp.max(score, axis=0, keepdims=True)
        weight = jnp.exp2(score - peak).astype(jnp.bfloat16)
        part = jnp.dot(blocks[block][1], weight, preferred_element_type=jnp.float32)
        parts[tile].append(part[:ROWS])
        peaks[tile].append(peak)
    return [with_peak(*merge(*pair)) for pair in zip(peaks, parts)]


def one_block(ones, slow, total):
    pieces = [ones[low * 2 + high][slow] for low in range(2) for high in range(2)]
    starts = [start_one(slow, high, low) for low in range(2) for high in range(2)]
    return block_of(pieces, starts, total)


def two_block(two, slow, total):
    return block_of(
        [two[piece] for piece in range(SUB)],
        [start_two(slow, piece) for piece in range(SUB)],
        total,
    )


def col_kernel(total, scale, *refs):
    ones, two, out = refs[:SUB], refs[SUB], refs[SUB + 1]
    query = jnp.concatenate([two[piece, :, :WIDTH] for piece in range(SUB)], axis=0)
    blocks = [one_block(ones, slow, total) for slow in range(SUB)]
    (out[...],) = attend(scale, [query], blocks)


def row_kernel(total, scale, halves, *refs):
    ones, twos, outs = refs[:2], refs[2 : 2 + SUB], refs[2 + SUB :]
    tiles = [
        jnp.concatenate(
            [
                ones[2 * core + high][slow, :, :WIDTH]
                for slow in (2 * half, 2 * half + 1)
                for high in range(2)
            ],
            axis=0,
        )
        for core, half in halves
    ]
    blocks = [two_block(two, block, total) for block, two in enumerate(twos)]
    wholes = attend(scale, tiles, blocks)
    for out in outs:
        for index in range(out.shape[0]):
            out[index] = wholes.pop(0)


def core_kernel(halves, *refs):
    (theirs, *mine), outs = refs[: -2 * len(halves)], refs[-2 * len(halves) :]
    for index, half in enumerate(halves):
        own = mine[0][index]
        whole = merged([own, theirs[half]])
        outs[2 * index][...] = whole[:, : 2 * SHARD]
        outs[2 * index + 1][...] = whole[:, 2 * SHARD :]


def chip_kernel(*refs):
    ins, (keep, send) = refs[:SUB], refs[SUB:]
    whole = merged([ref[...] for ref in ins])
    keep[...] = whole[:, :SHARD]
    send[...] = whole[:, SHARD:]


def block_kernel(*refs):
    ins, outs = refs[:SUB], refs[SUB:]
    for piece in range(SUB):
        span = slice(piece * SHARD, (piece + 1) * SHARD)
        outs[piece][...] = merged([ref[:, span] for ref in ins])


def finish_kernel(total, *refs):
    ins, outs = refs[:-4], refs[-4:]
    lane = lax.broadcasted_iota(jnp.int32, (1, SHARD), 1).astype(jnp.float32) / GRID_W
    for side, start in enumerate((start_one(0, 0, 0), start_two(0, 0))):
        matched, flow = outs[2 * side], outs[2 * side + 1]
        own_across, own_down = piece_coords(start, total)
        parts = [ref[...] for ref in (ins[2:] if side else ins[:2])]
        _, whole = merge([peak_of(part) for part in parts], parts)
        inverse = 1.0 / whole[WIDTH + TOTAL_ROW : WIDTH + TOTAL_ROW + 1, :]
        matched[...] = (whole[:WIDTH] * inverse).T
        across = whole[WIDTH + ACROSS_ROW : WIDTH + ACROSS_ROW + 1, :] * inverse
        down = whole[WIDTH + DOWN_ROW : WIDTH + DOWN_ROW + 1, :] * inverse
        flow[0:1, :] = across - (own_across + lane)
        flow[1:2, :] = down - own_down


def call(kernel, shapes, args, scratch=(), work=0, specs=None, vmem=48 << 20):
    moved = sum(math.prod(a.shape) * a.dtype.itemsize for a in (*args, *shapes))
    return pl.pallas_call(
        kernel,
        out_shape=shapes,
        in_specs=specs or [VMEM] * len(args),
        out_specs=[VMEM] * len(shapes),
        scratch_shapes=list(scratch),
        compiler_params=pltpu.CompilerParams(vmem_limit_bytes=vmem),
        cost_estimate=pl.CostEstimate(
            flops=4 * WIDTH * work, bytes_accessed=moved, transcendentals=work
        ),
    )(*args)


def together(values):
    return lax.optimization_barrier(values)


def f32(*shape):
    return jax.ShapeDtypeStruct(shape, jnp.float32)


def bf16(*shape):
    return jax.ShapeDtypeStruct(shape, jnp.bfloat16)


def body(feat_one, feat_two, value_one, value_two):
    total = feat_one.shape[0] * lax.axis_size("row") * lax.axis_size("col")
    scale = math.log2(math.e) / math.sqrt(WIDTH)
    packed = jax.ShapeDtypeStruct((SHARD, 2 * WIDTH), jnp.bfloat16)
    own_one, own_two = call(
        pack_kernel,
        [packed] * 2,
        (feat_one, value_one, feat_two, value_two),
        scratch=[
            pltpu.VMEM((2, SHARD, WIDTH), jnp.bfloat16),
            pltpu.SemaphoreType.DMA((4,)),
        ],
        specs=[HBM] * 4,
        vmem=62 << 20,
    )

    two = [own_two] + [fast_shift("row", own_two, -step) for step in range(1, SUB)]
    one = [own_one, fast_swap("col", own_one, 2)]
    one, two = together((jnp.stack(one), jnp.stack(two)))
    one = [one] + [slow_shift("col", one, -step) for step in range(1, SUB)]
    twos = [two] + [slow_shift("row", two, -step) for step in range(1, SUB)]
    one, twos = together((jnp.stack(one, axis=1), twos))
    other = fast_swap("col", one, 1)
    ones = [one[0], one[1], other[0], other[1]]

    def col_scores(*refs):
        col_kernel(total, scale, *refs)

    def row_scores(ones, twos, halves, weight, *counts):
        shapes = [f32(count, ROWS, BLOCK) for count in counts]
        kernel = functools.partial(row_kernel, total, scale, halves)
        return call(kernel, shapes, (*ones, *twos), work=weight * work)

    def core_merge(mine, theirs, *halves):
        shapes = [f32(ROWS, 2 * SHARD)] * (2 * len(halves))
        return call(functools.partial(core_kernel, halves), shapes, (theirs, mine))

    def spread(axis, parts, first=0):
        return [
            slow_shift(axis, part, first + step) if first + step else part
            for step, part in enumerate(parts)
        ]

    work = BLOCK * BLOCK * SUB
    cols = [None] * SUB
    (keep_one,) = row_scores(ones[:2], twos, ((0, 0), (0, 1)), 2, 2)
    (send_one,) = row_scores(ones[2:], twos, ((0, 0), (0, 1)), 2, 2)
    theirs_one = fast_swap("col", send_one, 1)
    ones, _ = together((ones, send_one))
    for step in (1, 3, 2, 0):
        (cols[step],) = call(col_scores, [f32(ROWS, BLOCK)], (*ones, twos[step]), work=work)
    cols = spread("row", cols)
    rows = spread("col", core_merge(keep_one, theirs_one, 0, 1))
    cols = call(block_kernel, [f32(ROWS, SHARD)] * SUB, cols, work=4 * work)
    cols = [cols[0]] + [fast_shift("row", cols[step], step) for step in range(1, SUB)]
    keep, send = call(chip_kernel, [f32(ROWS, SHARD)] * 2, rows)
    theirs = fast_swap("col", send, 2)
    outs = [f32(SHARD, WIDTH), f32(2, SHARD)] * 2
    return tuple(call(functools.partial(finish_kernel, total), outs, (keep, theirs, *cols)))


def solution(mesh):
    return jax.shard_map(
        body,
        mesh=mesh,
        in_specs=(
            P(("row", "col"), None),
            P(("col", "row"), None),
            P(("row", "col"), None),
            P(("col", "row"), None),
        ),
        out_specs=(
            P(("row", "col"), None),
            P(None, ("row", "col")),
            P(("col", "row"), None),
            P(None, ("col", "row")),
        ),
        check_vma=False,
    )
```

```python
import functools
import math

import jax
import jax.numpy as jnp
from jax import lax
from jax.experimental import pallas as pl
from jax.experimental.pallas import tpu as pltpu
from jax.sharding import PartitionSpec as P

GRID_W = 256
SUB = 4
SHARD = 128
WIDTH = 128
BLOCK = SUB * SHARD
ROWS = WIDTH + 8
AUG = 16
TOTAL_ROW, ACROSS_ROW, DOWN_ROW, PEAK_ROW = 0, 1, 2, 3
VMEM = pl.BlockSpec(memory_space=pltpu.VMEM)
HBM = pl.BlockSpec(memory_space=pltpu.HBM)


def slow_shift(axis, value, step):
    pairs = [(i, ((i // SUB + step) % SUB) * SUB + i % SUB) for i in range(SUB * SUB)]
    return lax.ppermute(value, axis, pairs)


def fast_shift(axis, value, step):
    pairs = [(i, (i // SUB) * SUB + (i % SUB + step) % SUB) for i in range(SUB * SUB)]
    return lax.ppermute(value, axis, pairs)


def fast_swap(axis, value, step):
    return lax.ppermute(value, axis, [(i, i ^ step) for i in range(SUB * SUB)])


def pack_kernel(feat_one, value_one, feat_two, value_two, out_one, out_two, held, sems):
    copies = [
        pltpu.make_async_copy(feat_one, out_one.at[:, :WIDTH], sems.at[0]),
        pltpu.make_async_copy(feat_two, out_two.at[:, :WIDTH], sems.at[1]),
        pltpu.make_async_copy(value_one, held.at[0], sems.at[2]),
        pltpu.make_async_copy(value_two, held.at[1], sems.at[3]),
    ]
    for copy in copies:
        copy.start()
    for side, out in ((0, out_one), (1, out_two)):
        copies[2 + side].wait()
        out[:, WIDTH:] = held[side].astype(jnp.float32).T.astype(jnp.bfloat16)
    copies[0].wait()
    copies[1].wait()


def piece_coords(start, total):
    across = (start % GRID_W).astype(jnp.float32) / GRID_W
    down = (start // GRID_W).astype(jnp.float32) / (total // GRID_W)
    return across, down


def coord_rows(start, total):
    across, down = piece_coords(start, total)
    sub = lax.broadcasted_iota(jnp.int32, (AUG, SHARD), 0)
    lane = lax.broadcasted_iota(jnp.int32, (AUG, SHARD), 1).astype(jnp.float32) / GRID_W
    rows = jnp.where(sub == DOWN_ROW, down, 0.0)
    rows = jnp.where(sub == ACROSS_ROW, across + lane, rows)
    rows = jnp.where(sub == TOTAL_ROW, 1.0, rows)
    return rows.astype(jnp.bfloat16)


def block_of(pieces, starts, total):
    keys = jnp.concatenate([piece[:, :WIDTH] for piece in pieces], axis=0)
    values = jnp.concatenate([piece[:, WIDTH:] for piece in pieces], axis=1)
    extra = jnp.concatenate([coord_rows(start, total) for start in starts], axis=1)
    return keys, jnp.concatenate([values, extra], axis=0)


def start_one(slow, fast_high, fast_low):
    row, col = lax.axis_index("row"), lax.axis_index("col")
    x = (col // SUB + slow) % SUB
    fast = (col % SUB) ^ (2 * fast_high + fast_low)
    return ((row * SUB + x) * SUB + fast) * SHARD


def start_two(slow, fast):
    row, col = lax.axis_index("row"), lax.axis_index("col")
    y = (row // SUB + slow) % SUB
    z = (row % SUB + fast) % SUB
    return ((col * SUB + y) * SUB + z) * SHARD


def merge(peaks, parts):
    top = peaks[0]
    for peak in peaks[1:]:
        top = jnp.maximum(top, peak)
    whole = None
    for peak, part in zip(peaks, parts):
        term = part * jnp.exp2(peak - top)
        whole = term if whole is None else whole + term
    return top, whole


def with_peak(top, whole):
    sub = lax.broadcasted_iota(jnp.int32, (ROWS - WIDTH, top.shape[1]), 0)
    return jnp.concatenate(
        [whole[:WIDTH], jnp.where(sub == PEAK_ROW, top, whole[WIDTH:])], axis=0
    )


def peak_of(part):
    return part[WIDTH + PEAK_ROW : WIDTH + PEAK_ROW + 1, :]


def merged(parts):
    return with_peak(*merge([peak_of(part) for part in parts], parts))


def attend(scale, queries, blocks):
    steps = [(tile, block) for tile in range(len(queries)) for block in range(len(blocks))]

    def raw(tile, block):
        return lax.dot_general(
            blocks[block][0],
            queries[tile],
            (((1,), (1,)), ((), ())),
            preferred_element_type=jnp.float32,
        )

    peaks, parts = [[] for _ in queries], [[] for _ in queries]
    ahead = raw(*steps[0])
    for at, (tile, block) in enumerate(steps):
        score = ahead * scale
        if at + 1 < len(steps):
            ahead = raw(*steps[at + 1])
        peak = jnp.max(score, axis=0, keepdims=True)
        weight = jnp.exp2(score - peak).astype(jnp.bfloat16)
        part = jnp.dot(blocks[block][1], weight, preferred_element_type=jnp.float32)
        parts[tile].append(part[:ROWS])
        peaks[tile].append(peak)
    return [with_peak(*merge(*pair)) for pair in zip(peaks, parts)]


def one_block(ones, slow, total):
    pieces = [ones[low * 2 + high][slow] for low in range(2) for high in range(2)]
    starts = [start_one(slow, high, low) for low in range(2) for high in range(2)]
    return block_of(pieces, starts, total)


def two_block(two, slow, total):
    return block_of(
        [two[piece] for piece in range(SUB)],
        [start_two(slow, piece) for piece in range(SUB)],
        total,
    )


def col_kernel(total, scale, count, *refs):
    ones, twos, outs = refs[:SUB], refs[SUB : SUB + count], refs[SUB + count :]
    tiles = [
        jnp.concatenate([two[piece, :, :WIDTH] for piece in range(SUB)], axis=0) for two in twos
    ]
    blocks = [one_block(ones, slow, total) for slow in range(SUB)]
    for out, whole in zip(outs, attend(scale, tiles, blocks)):
        out[...] = whole


def row_kernel(total, scale, halves, *refs):
    ones, twos, outs = refs[:2], refs[2 : 2 + SUB], refs[2 + SUB :]
    tiles = [
        jnp.concatenate(
            [
                ones[2 * core + high][slow, :, :WIDTH]
                for slow in (2 * half, 2 * half + 1)
                for high in range(2)
            ],
            axis=0,
        )
        for core, half in halves
    ]
    blocks = [two_block(two, block, total) for block, two in enumerate(twos)]
    wholes = attend(scale, tiles, blocks)
    for out in outs:
        for index in range(out.shape[0]):
            out[index] = wholes.pop(0)


def core_kernel(halves, *refs):
    (theirs, *mine), outs = refs[: -2 * len(halves)], refs[-2 * len(halves) :]
    for index, half in enumerate(halves):
        own = mine[0][index]
        whole = merged([own, theirs[half]])
        outs[2 * index][...] = whole[:, : 2 * SHARD]
        outs[2 * index + 1][...] = whole[:, 2 * SHARD :]


def chip_kernel(*refs):
    ins, (keep, send) = refs[:SUB], refs[SUB:]
    whole = merged([ref[...] for ref in ins])
    keep[...] = whole[:, :SHARD]
    send[...] = whole[:, SHARD:]


def block_kernel(*refs):
    ins, outs = refs[:SUB], refs[SUB:]
    for piece in range(SUB):
        span = slice(piece * SHARD, (piece + 1) * SHARD)
        outs[piece][...] = merged([ref[:, span] for ref in ins])


def finish_kernel(total, *refs):
    ins, outs = refs[:-4], refs[-4:]
    lane = lax.broadcasted_iota(jnp.int32, (1, SHARD), 1).astype(jnp.float32) / GRID_W
    for side, start in enumerate((start_one(0, 0, 0), start_two(0, 0))):
        matched, flow = outs[2 * side], outs[2 * side + 1]
        own_across, own_down = piece_coords(start, total)
        parts = [ref[...] for ref in (ins[2:] if side else ins[:2])]
        _, whole = merge([peak_of(part) for part in parts], parts)
        inverse = 1.0 / whole[WIDTH + TOTAL_ROW : WIDTH + TOTAL_ROW + 1, :]
        matched[...] = (whole[:WIDTH] * inverse).T
        across = whole[WIDTH + ACROSS_ROW : WIDTH + ACROSS_ROW + 1, :] * inverse
        down = whole[WIDTH + DOWN_ROW : WIDTH + DOWN_ROW + 1, :] * inverse
        flow[0:1, :] = across - (own_across + lane)
        flow[1:2, :] = down - own_down


def call(kernel, shapes, args, scratch=(), work=0, specs=None, vmem=48 << 20):
    moved = sum(math.prod(a.shape) * a.dtype.itemsize for a in (*args, *shapes))
    return pl.pallas_call(
        kernel,
        out_shape=shapes,
        in_specs=specs or [VMEM] * len(args),
        out_specs=[VMEM] * len(shapes),
        scratch_shapes=list(scratch),
        compiler_params=pltpu.CompilerParams(vmem_limit_bytes=vmem),
        cost_estimate=pl.CostEstimate(
            flops=4 * WIDTH * work, bytes_accessed=moved, transcendentals=work
        ),
    )(*args)


def together(values):
    return lax.optimization_barrier(values)


def f32(*shape):
    return jax.ShapeDtypeStruct(shape, jnp.float32)


def bf16(*shape):
    return jax.ShapeDtypeStruct(shape, jnp.bfloat16)


def body(feat_one, feat_two, value_one, value_two):
    total = feat_one.shape[0] * lax.axis_size("row") * lax.axis_size("col")
    scale = math.log2(math.e) / math.sqrt(WIDTH)
    packed = jax.ShapeDtypeStruct((SHARD, 2 * WIDTH), jnp.bfloat16)
    own_one, own_two = call(
        pack_kernel,
        [packed] * 2,
        (feat_one, value_one, feat_two, value_two),
        scratch=[
            pltpu.VMEM((2, SHARD, WIDTH), jnp.bfloat16),
            pltpu.SemaphoreType.DMA((4,)),
        ],
        specs=[HBM] * 4,
        vmem=62 << 20,
    )

    two = [own_two] + [fast_shift("row", own_two, -step) for step in range(1, SUB)]
    one = [own_one, fast_swap("col", own_one, 2)]
    one, two = together((jnp.stack(one), jnp.stack(two)))
    one = [one] + [slow_shift("col", one, -step) for step in range(1, SUB)]
    twos = [two] + [slow_shift("row", two, -step) for step in range(1, SUB)]
    one, twos = together((jnp.stack(one, axis=1), twos))
    other = fast_swap("col", one, 1)
    ones = [one[0], one[1], other[0], other[1]]

    def col_scores(*steps):
        kernel = functools.partial(col_kernel, total, scale, len(steps))
        args = (*ones, *(twos[step] for step in steps))
        return call(kernel, [f32(ROWS, BLOCK)] * len(steps), args, work=len(steps) * work)

    def row_scores(ones, twos, halves, weight, *counts):
        shapes = [f32(count, ROWS, BLOCK) for count in counts]
        kernel = functools.partial(row_kernel, total, scale, halves)
        return call(kernel, shapes, (*ones, *twos), work=weight * work)

    def core_merge(mine, theirs, *halves):
        shapes = [f32(ROWS, 2 * SHARD)] * (2 * len(halves))
        return call(functools.partial(core_kernel, halves), shapes, (theirs, mine))

    def spread(axis, parts, first=0):
        return [
            slow_shift(axis, part, first + step) if first + step else part
            for step, part in enumerate(parts)
        ]

    work = BLOCK * BLOCK * SUB
    cols = [None] * SUB
    mine = ones[:2]
    cols[2], cols[3], cols[1] = col_scores(2, 3, 1)
    ones, far = together((ones, cols[1:]))
    (cols[0],) = col_scores(0)
    cols = spread("row", [cols[0], *far])
    (send_one,) = row_scores(ones[2:], twos, ((0, 0), (0, 1)), 2, 2)
    theirs_one = fast_swap("col", send_one, 1)
    (keep_one,) = row_scores(ones[:2], twos, ((0, 0), (0, 1)), 2, 2)
    cols = call(block_kernel, [f32(ROWS, SHARD)] * SUB, cols, work=40 * work)
    theirs_one, cols = together((theirs_one, cols))
    cols = [cols[0]] + [fast_shift("row", cols[step], step) for step in range(1, SUB)]
    rows = spread("col", core_merge(keep_one, theirs_one, 0, 1))
    keep, send = call(chip_kernel, [f32(ROWS, SHARD)] * 2, rows)
    theirs = fast_swap("col", send, 2)
    outs = [f32(SHARD, WIDTH), f32(2, SHARD)] * 2
    return tuple(call(functools.partial(finish_kernel, total), outs, (keep, theirs, *cols)))


def solution(mesh):
    return jax.shard_map(
        body,
        mesh=mesh,
        in_specs=(
            P(("row", "col"), None),
            P(("col", "row"), None),
            P(("row", "col"), None),
            P(("col", "row"), None),
        ),
        out_specs=(
            P(("row", "col"), None),
            P(None, ("row", "col")),
            P(("col", "row"), None),
            P(None, ("col", "row")),
        ),
        check_vma=False,
    )
```

```python
import functools
import math

import jax
import jax.numpy as jnp
from jax import lax
from jax.experimental import pallas as pl
from jax.experimental.pallas import tpu as pltpu
from jax.sharding import PartitionSpec as P

GRID_W = 256
SUB = 4
SHARD = 128
WIDTH = 128
BLOCK = SUB * SHARD
ROWS = WIDTH + 8
AUG = 16
TOTAL_ROW, ACROSS_ROW, DOWN_ROW, PEAK_ROW = 0, 1, 2, 3
VMEM = pl.BlockSpec(memory_space=pltpu.VMEM)
HBM = pl.BlockSpec(memory_space=pltpu.HBM)


def slow_shift(axis, value, step):
    pairs = [(i, ((i // SUB + step) % SUB) * SUB + i % SUB) for i in range(SUB * SUB)]
    return lax.ppermute(value, axis, pairs)


def fast_shift(axis, value, step):
    pairs = [(i, (i // SUB) * SUB + (i % SUB + step) % SUB) for i in range(SUB * SUB)]
    return lax.ppermute(value, axis, pairs)


def fast_swap(axis, value, step):
    return lax.ppermute(value, axis, [(i, i ^ step) for i in range(SUB * SUB)])


def pack_kernel(feat_one, value_one, feat_two, value_two, out_one, out_two, held, sems):
    copies = [
        pltpu.make_async_copy(feat_one, out_one.at[:, :WIDTH], sems.at[0]),
        pltpu.make_async_copy(feat_two, out_two.at[:, :WIDTH], sems.at[1]),
        pltpu.make_async_copy(value_one, held.at[0], sems.at[2]),
        pltpu.make_async_copy(value_two, held.at[1], sems.at[3]),
    ]
    for copy in copies:
        copy.start()
    for side, out in ((0, out_one), (1, out_two)):
        copies[2 + side].wait()
        out[:, WIDTH:] = held[side].astype(jnp.float32).T.astype(jnp.bfloat16)
    copies[0].wait()
    copies[1].wait()


def piece_coords(start, total):
    across = (start % GRID_W).astype(jnp.float32) / GRID_W
    down = (start // GRID_W).astype(jnp.float32) / (total // GRID_W)
    return across, down


def coord_rows(start, total):
    across, down = piece_coords(start, total)
    sub = lax.broadcasted_iota(jnp.int32, (AUG, SHARD), 0)
    lane = lax.broadcasted_iota(jnp.int32, (AUG, SHARD), 1).astype(jnp.float32) / GRID_W
    rows = jnp.where(sub == DOWN_ROW, down, 0.0)
    rows = jnp.where(sub == ACROSS_ROW, across + lane, rows)
    rows = jnp.where(sub == TOTAL_ROW, 1.0, rows)
    return rows.astype(jnp.bfloat16)


def block_of(keys, values, starts, total):
    keys = jnp.concatenate(keys, axis=0)
    values = jnp.concatenate(values, axis=1)
    extra = jnp.concatenate([coord_rows(start, total) for start in starts], axis=1)
    return keys, jnp.concatenate([values, extra], axis=0)


def start_one(slow, fast_high, fast_low):
    row, col = lax.axis_index("row"), lax.axis_index("col")
    x = (col // SUB + slow) % SUB
    fast = (col % SUB) ^ (2 * fast_high + fast_low)
    return ((row * SUB + x) * SUB + fast) * SHARD


def start_two(slow, fast):
    row, col = lax.axis_index("row"), lax.axis_index("col")
    y = (row // SUB + slow) % SUB
    z = (row % SUB + fast) % SUB
    return ((col * SUB + y) * SUB + z) * SHARD


def merge(peaks, parts):
    top = peaks[0]
    for peak in peaks[1:]:
        top = jnp.maximum(top, peak)
    whole = None
    for peak, part in zip(peaks, parts):
        term = part * jnp.exp2(peak - top)
        whole = term if whole is None else whole + term
    return top, whole


def with_peak(top, whole):
    sub = lax.broadcasted_iota(jnp.int32, (ROWS - WIDTH, top.shape[1]), 0)
    return jnp.concatenate(
        [whole[:WIDTH], jnp.where(sub == PEAK_ROW, top, whole[WIDTH:])], axis=0
    )


def peak_of(part):
    return part[WIDTH + PEAK_ROW : WIDTH + PEAK_ROW + 1, :]


def merged(parts):
    return with_peak(*merge([peak_of(part) for part in parts], parts))


def attend(scale, queries, blocks):
    steps = [(tile, block) for tile in range(len(queries)) for block in range(len(blocks))]

    def raw(tile, block):
        return lax.dot_general(
            blocks[block][0],
            queries[tile],
            (((1,), (1,)), ((), ())),
            preferred_element_type=jnp.float32,
        )

    peaks, parts = [[] for _ in queries], [[] for _ in queries]
    ahead = raw(*steps[0])
    for at, (tile, block) in enumerate(steps):
        score = ahead * scale
        if at + 1 < len(steps):
            ahead = raw(*steps[at + 1])
        peak = jnp.max(score, axis=0, keepdims=True)
        weight = jnp.exp2(score - peak).astype(jnp.bfloat16)
        part = jnp.dot(blocks[block][1], weight, preferred_element_type=jnp.float32)
        parts[tile].append(part[:ROWS])
        peaks[tile].append(peak)
    return [with_peak(*merge(*pair)) for pair in zip(peaks, parts)]


def one_block(ones, slow, total):
    pieces = [ones[low * 2 + high][slow] for low in range(2) for high in range(2)]
    starts = [start_one(slow, high, low) for low in range(2) for high in range(2)]
    keys, values = [p[:, :WIDTH] for p in pieces], [p[:, WIDTH:] for p in pieces]
    return block_of(keys, values, starts, total)


def two_block(two, vals, slow, total):
    return block_of(
        [two[piece] for piece in range(SUB)],
        [vals[piece] for piece in range(SUB)],
        [start_two(slow, piece) for piece in range(SUB)],
        total,
    )


def col_kernel(total, scale, count, *refs):
    ones, twos, outs = refs[:SUB], refs[SUB : SUB + count], refs[SUB + count :]
    tiles = [
        jnp.concatenate([two[piece] for piece in range(SUB)], axis=0) for two in twos
    ]
    blocks = [one_block(ones, slow, total) for slow in range(SUB)]
    for out, whole in zip(outs, attend(scale, tiles, blocks)):
        out[...] = whole


def row_kernel(total, scale, halves, *refs):
    ones, twos, outs = refs[:2], refs[2 : 2 + 2 * SUB], refs[2 + 2 * SUB :]
    tiles = [
        jnp.concatenate(
            [
                ones[2 * core + high][slow, :, :WIDTH]
                for slow in (2 * half, 2 * half + 1)
                for high in range(2)
            ],
            axis=0,
        )
        for core, half in halves
    ]
    blocks = [two_block(twos[at], twos[SUB + at], at, total) for at in range(SUB)]
    wholes = attend(scale, tiles, blocks)
    for out in outs:
        for index in range(out.shape[0]):
            out[index] = wholes.pop(0)


def core_kernel(halves, *refs):
    (theirs, *mine), outs = refs[: -2 * len(halves)], refs[-2 * len(halves) :]
    for index, half in enumerate(halves):
        own = mine[0][index]
        whole = merged([own, theirs[half]])
        outs[2 * index][...] = whole[:, : 2 * SHARD]
        outs[2 * index + 1][...] = whole[:, 2 * SHARD :]


def chip_kernel(*refs):
    ins, (keep, send) = refs[:SUB], refs[SUB:]
    whole = merged([ref[...] for ref in ins])
    keep[...] = whole[:, :SHARD]
    send[...] = whole[:, SHARD:]


def block_kernel(*refs):
    ins, outs = refs[:SUB], refs[SUB:]
    for piece in range(SUB):
        span = slice(piece * SHARD, (piece + 1) * SHARD)
        outs[piece][...] = merged([ref[:, span] for ref in ins])


def finish_kernel(total, *refs):
    ins, outs = refs[:-4], refs[-4:]
    lane = lax.broadcasted_iota(jnp.int32, (1, SHARD), 1).astype(jnp.float32) / GRID_W
    for side, start in enumerate((start_one(0, 0, 0), start_two(0, 0))):
        matched, flow = outs[2 * side], outs[2 * side + 1]
        own_across, own_down = piece_coords(start, total)
        parts = [ref[...] for ref in (ins[2:] if side else ins[:2])]
        _, whole = merge([peak_of(part) for part in parts], parts)
        inverse = 1.0 / whole[WIDTH + TOTAL_ROW : WIDTH + TOTAL_ROW + 1, :]
        matched[...] = (whole[:WIDTH] * inverse).T
        across = whole[WIDTH + ACROSS_ROW : WIDTH + ACROSS_ROW + 1, :] * inverse
        down = whole[WIDTH + DOWN_ROW : WIDTH + DOWN_ROW + 1, :] * inverse
        flow[0:1, :] = across - (own_across + lane)
        flow[1:2, :] = down - own_down


def call(kernel, shapes, args, scratch=(), work=0, specs=None, vmem=48 << 20):
    moved = sum(math.prod(a.shape) * a.dtype.itemsize for a in (*args, *shapes))
    return pl.pallas_call(
        kernel,
        out_shape=shapes,
        in_specs=specs or [VMEM] * len(args),
        out_specs=[VMEM] * len(shapes),
        scratch_shapes=list(scratch),
        compiler_params=pltpu.CompilerParams(vmem_limit_bytes=vmem),
        cost_estimate=pl.CostEstimate(
            flops=4 * WIDTH * work, bytes_accessed=moved, transcendentals=work
        ),
    )(*args)


def together(values):
    return lax.optimization_barrier(values)


def f32(*shape):
    return jax.ShapeDtypeStruct(shape, jnp.float32)


def bf16(*shape):
    return jax.ShapeDtypeStruct(shape, jnp.bfloat16)


def body(feat_one, feat_two, value_one, value_two):
    total = feat_one.shape[0] * lax.axis_size("row") * lax.axis_size("col")
    order = (2, 3, 1)
    scale = math.log2(math.e) / math.sqrt(WIDTH)
    packed = jax.ShapeDtypeStruct((SHARD, 2 * WIDTH), jnp.bfloat16)
    own_one, own_two = call(
        pack_kernel,
        [packed] * 2,
        (feat_one, value_one, feat_two, value_two),
        scratch=[
            pltpu.VMEM((2, SHARD, WIDTH), jnp.bfloat16),
            pltpu.SemaphoreType.DMA((4,)),
        ],
        specs=[HBM] * 4,
        vmem=62 << 20,
    )

    two = [own_two] + [fast_shift("row", own_two, -step) for step in range(1, SUB)]
    one = [own_one, fast_swap("col", own_one, 2)]
    one, two = together((jnp.stack(one), jnp.stack(two)))
    one = [one] + [slow_shift("col", one, -step) for step in range(1, SUB)]
    vals = two[:, :, WIDTH:]
    twos = [two[:, :, :WIDTH]]
    twos += [slow_shift("row", twos[0], -step) for step in order]
    one, twos, vals = together((jnp.stack(one, axis=1), twos, vals))
    twos = [twos[0]] + [twos[1 + order.index(step)] for step in range(1, SUB)]
    other = fast_swap("col", one, 1)
    vals = [vals] + [slow_shift("row", vals, -step) for step in range(1, SUB)]
    ones = [one[0], one[1], other[0], other[1]]

    def col_scores(*steps):
        kernel = functools.partial(col_kernel, total, scale, len(steps))
        args = (*ones, *(twos[step] for step in steps))
        return call(kernel, [f32(ROWS, BLOCK)] * len(steps), args, work=len(steps) * work)

    def row_scores(ones, twos, halves, weight, *counts):
        shapes = [f32(count, ROWS, BLOCK) for count in counts]
        kernel = functools.partial(row_kernel, total, scale, halves)
        return call(kernel, shapes, (*ones, *twos, *vals), work=weight * work)

    def core_merge(mine, theirs, *halves):
        shapes = [f32(ROWS, 2 * SHARD)] * (2 * len(halves))
        return call(functools.partial(core_kernel, halves), shapes, (theirs, mine))

    def spread(axis, parts, first=0):
        return [
            slow_shift(axis, part, first + step) if first + step else part
            for step, part in enumerate(parts)
        ]

    work = BLOCK * BLOCK * SUB
    cols = [None] * SUB
    mine = ones[:2]
    cols[2], cols[3], cols[1] = col_scores(2, 3, 1)
    ones, far = together((ones, cols[1:]))
    (cols[0],) = col_scores(0)
    cols = spread("row", [cols[0], *far])
    (send_one,) = row_scores(ones[2:], twos, ((0, 0), (0, 1)), 2, 2)
    theirs_one = fast_swap("col", send_one, 1)
    (keep_one,) = row_scores(ones[:2], twos, ((0, 0), (0, 1)), 2, 2)
    cols = call(block_kernel, [f32(ROWS, SHARD)] * SUB, cols, work=40 * work)
    theirs_one, cols = together((theirs_one, cols))
    cols = [cols[0]] + [fast_shift("row", cols[step], step) for step in range(1, SUB)]
    rows = spread("col", core_merge(keep_one, theirs_one, 0, 1))
    keep, send = call(chip_kernel, [f32(ROWS, SHARD)] * 2, rows)
    theirs = fast_swap("col", send, 2)
    outs = [f32(SHARD, WIDTH), f32(2, SHARD)] * 2
    return tuple(call(functools.partial(finish_kernel, total), outs, (keep, theirs, *cols)))


def solution(mesh):
    return jax.shard_map(
        body,
        mesh=mesh,
        in_specs=(
            P(("row", "col"), None),
            P(("col", "row"), None),
            P(("row", "col"), None),
            P(("col", "row"), None),
        ),
        out_specs=(
            P(("row", "col"), None),
            P(None, ("row", "col")),
            P(("col", "row"), None),
            P(None, ("col", "row")),
        ),
        check_vma=False,
    )
```

```python
import functools
import math

import jax
import jax.numpy as jnp
from jax import lax
from jax.experimental import pallas as pl
from jax.experimental.pallas import tpu as pltpu
from jax.sharding import PartitionSpec as P

GRID_W = 256
SUB = 4
SHARD = 128
WIDTH = 128
BLOCK = SUB * SHARD
ROWS = WIDTH + 8
AUG = 16
TOTAL_ROW, ACROSS_ROW, DOWN_ROW, PEAK_ROW = 0, 1, 2, 3
VMEM = pl.BlockSpec(memory_space=pltpu.VMEM)
HBM = pl.BlockSpec(memory_space=pltpu.HBM)


def slow_shift(axis, value, step):
    pairs = [(i, ((i // SUB + step) % SUB) * SUB + i % SUB) for i in range(SUB * SUB)]
    return lax.ppermute(value, axis, pairs)


def fast_shift(axis, value, step):
    pairs = [(i, (i // SUB) * SUB + (i % SUB + step) % SUB) for i in range(SUB * SUB)]
    return lax.ppermute(value, axis, pairs)


def fast_swap(axis, value, step):
    return lax.ppermute(value, axis, [(i, i ^ step) for i in range(SUB * SUB)])


def pack_kernel(feat_one, value_one, feat_two, value_two, out_one, out_two, held, sems):
    copies = [
        pltpu.make_async_copy(feat_one, out_one.at[:, :WIDTH], sems.at[0]),
        pltpu.make_async_copy(feat_two, out_two.at[:, :WIDTH], sems.at[1]),
        pltpu.make_async_copy(value_one, held.at[0], sems.at[2]),
        pltpu.make_async_copy(value_two, held.at[1], sems.at[3]),
    ]
    for copy in copies:
        copy.start()
    for side, out in ((0, out_one), (1, out_two)):
        copies[2 + side].wait()
        out[:, WIDTH:] = held[side].astype(jnp.float32).T.astype(jnp.bfloat16)
    copies[0].wait()
    copies[1].wait()


def piece_coords(start, total):
    across = (start % GRID_W).astype(jnp.float32) / GRID_W
    down = (start // GRID_W).astype(jnp.float32) / (total // GRID_W)
    return across, down


def coord_rows(start, total):
    across, down = piece_coords(start, total)
    sub = lax.broadcasted_iota(jnp.int32, (AUG, SHARD), 0)
    lane = lax.broadcasted_iota(jnp.int32, (AUG, SHARD), 1).astype(jnp.float32) / GRID_W
    rows = jnp.where(sub == DOWN_ROW, down, 0.0)
    rows = jnp.where(sub == ACROSS_ROW, across + lane, rows)
    rows = jnp.where(sub == TOTAL_ROW, 1.0, rows)
    return rows.astype(jnp.bfloat16)


def block_of(pieces, starts, total):
    keys = jnp.concatenate([piece[:, :WIDTH] for piece in pieces], axis=0)
    values = jnp.concatenate([piece[:, WIDTH:] for piece in pieces], axis=1)
    extra = jnp.concatenate([coord_rows(start, total) for start in starts], axis=1)
    return keys, jnp.concatenate([values, extra], axis=0)


def start_one(slow, fast_high, fast_low):
    row, col = lax.axis_index("row"), lax.axis_index("col")
    x = (col // SUB + slow) % SUB
    fast = (col % SUB) ^ (2 * fast_high + fast_low)
    return ((row * SUB + x) * SUB + fast) * SHARD


def start_two(slow, fast):
    row, col = lax.axis_index("row"), lax.axis_index("col")
    y = (row // SUB + slow) % SUB
    z = (row % SUB + fast) % SUB
    return ((col * SUB + y) * SUB + z) * SHARD


def merge(peaks, parts):
    top = peaks[0]
    for peak in peaks[1:]:
        top = jnp.maximum(top, peak)
    whole = None
    for peak, part in zip(peaks, parts):
        term = part * jnp.exp2(peak - top)
        whole = term if whole is None else whole + term
    return top, whole


def with_peak(top, whole):
    sub = lax.broadcasted_iota(jnp.int32, (ROWS - WIDTH, top.shape[1]), 0)
    return jnp.concatenate(
        [whole[:WIDTH], jnp.where(sub == PEAK_ROW, top, whole[WIDTH:])], axis=0
    )


def peak_of(part):
    return part[WIDTH + PEAK_ROW : WIDTH + PEAK_ROW + 1, :]


def merged(parts):
    return with_peak(*merge([peak_of(part) for part in parts], parts))


def attend(scale, queries, blocks):
    steps = [(tile, block) for tile in range(len(queries)) for block in range(len(blocks))]

    def raw(tile, block):
        return lax.dot_general(
            blocks[block][0],
            queries[tile],
            (((1,), (1,)), ((), ())),
            preferred_element_type=jnp.float32,
        )

    peaks, parts = [[] for _ in queries], [[] for _ in queries]
    ahead = raw(*steps[0])
    for at, (tile, block) in enumerate(steps):
        score = ahead * scale
        if at + 1 < len(steps):
            ahead = raw(*steps[at + 1])
        peak = jnp.max(score, axis=0, keepdims=True)
        weight = jnp.exp2(score - peak).astype(jnp.bfloat16)
        part = jnp.dot(blocks[block][1], weight, preferred_element_type=jnp.float32)
        parts[tile].append(part[:ROWS])
        peaks[tile].append(peak)
    return [with_peak(*merge(*pair)) for pair in zip(peaks, parts)]


def one_block(ones, slow, total):
    pieces = [ones[low * 2 + high][slow] for low in range(2) for high in range(2)]
    starts = [start_one(slow, high, low) for low in range(2) for high in range(2)]
    return block_of(pieces, starts, total)


def two_block(two, slow, total):
    return block_of(
        [two[piece] for piece in range(SUB)],
        [start_two(slow, piece) for piece in range(SUB)],
        total,
    )


def col_kernel(total, scale, count, *refs):
    ones, twos, outs = refs[:SUB], refs[SUB : SUB + count], refs[SUB + count :]
    tiles = [
        jnp.concatenate([two[piece, :, :WIDTH] for piece in range(SUB)], axis=0) for two in twos
    ]
    blocks = [one_block(ones, slow, total) for slow in range(SUB)]
    for out, whole in zip(outs, attend(scale, tiles, blocks)):
        out[...] = whole


def row_kernel(total, scale, halves, *refs):
    ones, twos, outs = refs[:2], refs[2 : 2 + SUB], refs[2 + SUB :]
    tiles = [
        jnp.concatenate(
            [
                ones[2 * core + high][slow, :, :WIDTH]
                for slow in (2 * half, 2 * half + 1)
                for high in range(2)
            ],
            axis=0,
        )
        for core, half in halves
    ]
    blocks = [two_block(two, block, total) for block, two in enumerate(twos)]
    wholes = attend(scale, tiles, blocks)
    for out in outs:
        for index in range(out.shape[0]):
            out[index] = wholes.pop(0)


def core_kernel(halves, *refs):
    (theirs, *mine), outs = refs[: -2 * len(halves)], refs[-2 * len(halves) :]
    for index, half in enumerate(halves):
        own = mine[0][index]
        whole = merged([own, theirs[half]])
        outs[2 * index][...] = whole[:, : 2 * SHARD]
        outs[2 * index + 1][...] = whole[:, 2 * SHARD :]


def chip_kernel(*refs):
    ins, (keep, send) = refs[:SUB], refs[SUB:]
    whole = merged([ref[...] for ref in ins])
    keep[...] = whole[:, :SHARD]
    send[...] = whole[:, SHARD:]


def block_kernel(*refs):
    ins, outs = refs[:SUB], refs[SUB:]
    for piece in range(SUB):
        span = slice(piece * SHARD, (piece + 1) * SHARD)
        outs[piece][...] = merged([ref[:, span] for ref in ins])


def finish_kernel(total, *refs):
    ins, outs = refs[:-4], refs[-4:]
    lane = lax.broadcasted_iota(jnp.int32, (1, SHARD), 1).astype(jnp.float32) / GRID_W
    for side, start in enumerate((start_one(0, 0, 0), start_two(0, 0))):
        matched, flow = outs[2 * side], outs[2 * side + 1]
        own_across, own_down = piece_coords(start, total)
        parts = [ref[...] for ref in (ins[2:] if side else ins[:2])]
        _, whole = merge([peak_of(part) for part in parts], parts)
        inverse = 1.0 / whole[WIDTH + TOTAL_ROW : WIDTH + TOTAL_ROW + 1, :]
        matched[...] = (whole[:WIDTH] * inverse).T
        across = whole[WIDTH + ACROSS_ROW : WIDTH + ACROSS_ROW + 1, :] * inverse
        down = whole[WIDTH + DOWN_ROW : WIDTH + DOWN_ROW + 1, :] * inverse
        flow[0:1, :] = across - (own_across + lane)
        flow[1:2, :] = down - own_down


def call(kernel, shapes, args, scratch=(), work=0, specs=None, vmem=48 << 20):
    moved = sum(math.prod(a.shape) * a.dtype.itemsize for a in (*args, *shapes))
    return pl.pallas_call(
        kernel,
        out_shape=shapes,
        in_specs=specs or [VMEM] * len(args),
        out_specs=[VMEM] * len(shapes),
        scratch_shapes=list(scratch),
        compiler_params=pltpu.CompilerParams(vmem_limit_bytes=vmem),
        cost_estimate=pl.CostEstimate(
            flops=4 * WIDTH * work, bytes_accessed=moved, transcendentals=work
        ),
    )(*args)


def together(values):
    return lax.optimization_barrier(values)


def f32(*shape):
    return jax.ShapeDtypeStruct(shape, jnp.float32)


def bf16(*shape):
    return jax.ShapeDtypeStruct(shape, jnp.bfloat16)


def body(feat_one, feat_two, value_one, value_two):
    total = feat_one.shape[0] * lax.axis_size("row") * lax.axis_size("col")
    scale = math.log2(math.e) / math.sqrt(WIDTH)
    packed = jax.ShapeDtypeStruct((SHARD, 2 * WIDTH), jnp.bfloat16)
    own_one, own_two = call(
        pack_kernel,
        [packed] * 2,
        (feat_one, value_one, feat_two, value_two),
        scratch=[
            pltpu.VMEM((2, SHARD, WIDTH), jnp.bfloat16),
            pltpu.SemaphoreType.DMA((4,)),
        ],
        specs=[HBM] * 4,
        vmem=62 << 20,
    )

    two = [own_two] + [fast_shift("row", own_two, -step) for step in range(1, SUB)]
    one = [own_one, fast_swap("col", own_one, 2)]
    one, two = together((jnp.stack(one), jnp.stack(two)))
    one = [one] + [slow_shift("col", one, -step) for step in range(1, SUB)]
    order = (3, 2, 1)
    twos = [two] + [slow_shift("row", two, -step) for step in order]
    one, twos = together((jnp.stack(one, axis=1), twos))
    twos = [twos[0]] + [twos[1 + order.index(step)] for step in range(1, SUB)]
    other = fast_swap("col", one, 1)
    ones = [one[0], one[1], other[0], other[1]]

    def col_scores(*steps):
        kernel = functools.partial(col_kernel, total, scale, len(steps))
        args = (*ones, *(twos[step] for step in steps))
        return call(kernel, [f32(ROWS, BLOCK)] * len(steps), args, work=len(steps) * work)

    def row_scores(ones, twos, halves, weight, *counts):
        shapes = [f32(count, ROWS, BLOCK) for count in counts]
        kernel = functools.partial(row_kernel, total, scale, halves)
        return call(kernel, shapes, (*ones, *twos), work=weight * work)

    def core_merge(mine, theirs, *halves):
        shapes = [f32(ROWS, 2 * SHARD)] * (2 * len(halves))
        return call(functools.partial(core_kernel, halves), shapes, (theirs, mine))

    def spread(axis, parts, first=0):
        return [
            slow_shift(axis, part, first + step) if first + step else part
            for step, part in enumerate(parts)
        ]

    work = BLOCK * BLOCK * SUB
    cols = [None] * SUB
    mine = ones[:2]
    cols[2], cols[3], cols[1] = col_scores(2, 3, 1)
    ones, far = together((ones, cols[1:]))
    (cols[0],) = col_scores(0)
    cols = spread("row", [cols[0], *far])
    (send_one,) = row_scores(ones[2:], twos, ((0, 0), (0, 1)), 2, 2)
    theirs_one = fast_swap("col", send_one, 1)
    (keep_one,) = row_scores(ones[:2], twos, ((0, 0), (0, 1)), 40, 2)
    cols = call(block_kernel, [f32(ROWS, SHARD)] * SUB, cols, work=1 * work)
    cols = [cols[0]] + [fast_shift("row", cols[step], step) for step in range(1, SUB)]
    rows = spread("col", core_merge(keep_one, theirs_one, 0, 1))
    keep, send = call(chip_kernel, [f32(ROWS, SHARD)] * 2, rows)
    theirs = fast_swap("col", send, 2)
    outs = [f32(SHARD, WIDTH), f32(2, SHARD)] * 2
    return tuple(call(functools.partial(finish_kernel, total), outs, (keep, theirs, *cols)))


def solution(mesh):
    return jax.shard_map(
        body,
        mesh=mesh,
        in_specs=(
            P(("row", "col"), None),
            P(("col", "row"), None),
            P(("row", "col"), None),
            P(("col", "row"), None),
        ),
        out_specs=(
            P(("row", "col"), None),
            P(None, ("row", "col")),
            P(("col", "row"), None),
            P(None, ("col", "row")),
        ),
        check_vma=False,
    )
```

```python
import functools
import math

import jax
import jax.numpy as jnp
from jax import lax
from jax.experimental import pallas as pl
from jax.experimental.pallas import tpu as pltpu
from jax.sharding import PartitionSpec as P

GRID_W = 256
SUB = 4
SHARD = 128
WIDTH = 128
BLOCK = SUB * SHARD
ROWS = WIDTH + 8
AUG = 16
TOTAL_ROW, ACROSS_ROW, DOWN_ROW, PEAK_ROW = 0, 1, 2, 3
VMEM = pl.BlockSpec(memory_space=pltpu.VMEM)
HBM = pl.BlockSpec(memory_space=pltpu.HBM)


def slow_shift(axis, value, step):
    pairs = [(i, ((i // SUB + step) % SUB) * SUB + i % SUB) for i in range(SUB * SUB)]
    return lax.ppermute(value, axis, pairs)


def fast_shift(axis, value, step):
    pairs = [(i, (i // SUB) * SUB + (i % SUB + step) % SUB) for i in range(SUB * SUB)]
    return lax.ppermute(value, axis, pairs)


def fast_swap(axis, value, step):
    return lax.ppermute(value, axis, [(i, i ^ step) for i in range(SUB * SUB)])


def pack_kernel(feat_one, value_one, feat_two, value_two, out_one, out_two, held, sems):
    copies = [
        pltpu.make_async_copy(feat_one, out_one.at[:, :WIDTH], sems.at[0]),
        pltpu.make_async_copy(feat_two, out_two.at[:, :WIDTH], sems.at[1]),
        pltpu.make_async_copy(value_one, held.at[0], sems.at[2]),
        pltpu.make_async_copy(value_two, held.at[1], sems.at[3]),
    ]
    for copy in copies:
        copy.start()
    for side, out in ((0, out_one), (1, out_two)):
        copies[2 + side].wait()
        out[:, WIDTH:] = held[side].astype(jnp.float32).T.astype(jnp.bfloat16)
    copies[0].wait()
    copies[1].wait()


def piece_coords(start, total):
    across = (start % GRID_W).astype(jnp.float32) / GRID_W
    down = (start // GRID_W).astype(jnp.float32) / (total // GRID_W)
    return across, down


def coord_rows(start, total):
    across, down = piece_coords(start, total)
    sub = lax.broadcasted_iota(jnp.int32, (AUG, SHARD), 0)
    lane = lax.broadcasted_iota(jnp.int32, (AUG, SHARD), 1).astype(jnp.float32) / GRID_W
    rows = jnp.where(sub == DOWN_ROW, down, 0.0)
    rows = jnp.where(sub == ACROSS_ROW, across + lane, rows)
    rows = jnp.where(sub == TOTAL_ROW, 1.0, rows)
    return rows.astype(jnp.bfloat16)


def block_of(pieces, starts, total):
    keys = jnp.concatenate([piece[:, :WIDTH] for piece in pieces], axis=0)
    values = jnp.concatenate([piece[:, WIDTH:] for piece in pieces], axis=1)
    extra = jnp.concatenate([coord_rows(start, total) for start in starts], axis=1)
    return keys, jnp.concatenate([values, extra], axis=0)


def start_one(slow, fast_high, fast_low):
    row, col = lax.axis_index("row"), lax.axis_index("col")
    x = (col // SUB + slow) % SUB
    fast = (col % SUB) ^ (2 * fast_high + fast_low)
    return ((row * SUB + x) * SUB + fast) * SHARD


def start_two(slow, fast):
    row, col = lax.axis_index("row"), lax.axis_index("col")
    y = (row // SUB + slow) % SUB
    z = (row % SUB + fast) % SUB
    return ((col * SUB + y) * SUB + z) * SHARD


def merge(peaks, parts):
    top = peaks[0]
    for peak in peaks[1:]:
        top = jnp.maximum(top, peak)
    whole = None
    for peak, part in zip(peaks, parts):
        term = part * jnp.exp2(peak - top)
        whole = term if whole is None else whole + term
    return top, whole


def with_peak(top, whole):
    sub = lax.broadcasted_iota(jnp.int32, (ROWS - WIDTH, top.shape[1]), 0)
    return jnp.concatenate(
        [whole[:WIDTH], jnp.where(sub == PEAK_ROW, top, whole[WIDTH:])], axis=0
    )


def peak_of(part):
    return part[WIDTH + PEAK_ROW : WIDTH + PEAK_ROW + 1, :]


def merged(parts):
    return with_peak(*merge([peak_of(part) for part in parts], parts))


def attend(scale, queries, blocks):
    steps = [(tile, block) for tile in range(len(queries)) for block in range(len(blocks))]

    def raw(tile, block):
        return lax.dot_general(
            blocks[block][0],
            queries[tile],
            (((1,), (1,)), ((), ())),
            preferred_element_type=jnp.float32,
        )

    peaks, parts = [[] for _ in queries], [[] for _ in queries]
    ahead = raw(*steps[0])
    for at, (tile, block) in enumerate(steps):
        score = ahead * scale
        if at + 1 < len(steps):
            ahead = raw(*steps[at + 1])
        peak = jnp.max(score, axis=0, keepdims=True)
        weight = jnp.exp2(score - peak).astype(jnp.bfloat16)
        part = jnp.dot(blocks[block][1], weight, preferred_element_type=jnp.float32)
        parts[tile].append(part[:ROWS])
        peaks[tile].append(peak)
    return [with_peak(*merge(*pair)) for pair in zip(peaks, parts)]


def one_block(ones, slow, total):
    pieces = [ones[low * 2 + high][slow] for low in range(2) for high in range(2)]
    starts = [start_one(slow, high, low) for low in range(2) for high in range(2)]
    return block_of(pieces, starts, total)


def two_block(two, slow, total):
    return block_of(
        [two[piece] for piece in range(SUB)],
        [start_two(slow, piece) for piece in range(SUB)],
        total,
    )


def col_kernel(total, scale, count, *refs):
    ones, twos, outs = refs[:SUB], refs[SUB : SUB + count], refs[SUB + count :]
    tiles = [
        jnp.concatenate([two[piece, :, :WIDTH] for piece in range(SUB)], axis=0) for two in twos
    ]
    blocks = [one_block(ones, slow, total) for slow in range(SUB)]
    for out, whole in zip(outs, attend(scale, tiles, blocks)):
        out[...] = whole


def row_kernel(total, scale, halves, *refs):
    ones, twos, outs = refs[:2], refs[2 : 2 + SUB], refs[2 + SUB :]
    tiles = [
        jnp.concatenate(
            [
                ones[2 * core + high][slow, :, :WIDTH]
                for slow in (2 * half, 2 * half + 1)
                for high in range(2)
            ],
            axis=0,
        )
        for core, half in halves
    ]
    blocks = [two_block(two, block, total) for block, two in enumerate(twos)]
    wholes = attend(scale, tiles, blocks)
    for out in outs:
        for index in range(out.shape[0]):
            out[index] = wholes.pop(0)


def core_kernel(halves, *refs):
    (theirs, *mine), outs = refs[: -2 * len(halves)], refs[-2 * len(halves) :]
    for index, half in enumerate(halves):
        own = mine[0][index]
        whole = merged([own, theirs[half]])
        outs[2 * index][...] = whole[:, : 2 * SHARD]
        outs[2 * index + 1][...] = whole[:, 2 * SHARD :]


def chip_kernel(*refs):
    ins, (keep, send) = refs[:SUB], refs[SUB:]
    whole = merged([ref[...] for ref in ins])
    keep[...] = whole[:, :SHARD]
    send[...] = whole[:, SHARD:]


def block_kernel(*refs):
    ins, outs = refs[:SUB], refs[SUB:]
    for piece in range(SUB):
        span = slice(piece * SHARD, (piece + 1) * SHARD)
        outs[piece][...] = merged([ref[:, span] for ref in ins])


def finish_kernel(total, *refs):
    ins, outs = refs[:-4], refs[-4:]
    lane = lax.broadcasted_iota(jnp.int32, (1, SHARD), 1).astype(jnp.float32) / GRID_W
    for side, start in enumerate((start_one(0, 0, 0), start_two(0, 0))):
        matched, flow = outs[2 * side], outs[2 * side + 1]
        own_across, own_down = piece_coords(start, total)
        parts = [ref[...] for ref in (ins[2:] if side else ins[:2])]
        _, whole = merge([peak_of(part) for part in parts], parts)
        inverse = 1.0 / whole[WIDTH + TOTAL_ROW : WIDTH + TOTAL_ROW + 1, :]
        matched[...] = (whole[:WIDTH] * inverse).T
        across = whole[WIDTH + ACROSS_ROW : WIDTH + ACROSS_ROW + 1, :] * inverse
        down = whole[WIDTH + DOWN_ROW : WIDTH + DOWN_ROW + 1, :] * inverse
        flow[0:1, :] = across - (own_across + lane)
        flow[1:2, :] = down - own_down


def call(kernel, shapes, args, scratch=(), work=0, specs=None, vmem=48 << 20):
    moved = sum(math.prod(a.shape) * a.dtype.itemsize for a in (*args, *shapes))
    return pl.pallas_call(
        kernel,
        out_shape=shapes,
        in_specs=specs or [VMEM] * len(args),
        out_specs=[VMEM] * len(shapes),
        scratch_shapes=list(scratch),
        compiler_params=pltpu.CompilerParams(vmem_limit_bytes=vmem),
        cost_estimate=pl.CostEstimate(
            flops=4 * WIDTH * work, bytes_accessed=moved, transcendentals=work
        ),
    )(*args)


def together(values):
    return lax.optimization_barrier(values)


def f32(*shape):
    return jax.ShapeDtypeStruct(shape, jnp.float32)


def bf16(*shape):
    return jax.ShapeDtypeStruct(shape, jnp.bfloat16)


def body(feat_one, feat_two, value_one, value_two):
    total = feat_one.shape[0] * lax.axis_size("row") * lax.axis_size("col")
    scale = math.log2(math.e) / math.sqrt(WIDTH)
    packed = jax.ShapeDtypeStruct((SHARD, 2 * WIDTH), jnp.bfloat16)
    own_one, own_two = call(
        pack_kernel,
        [packed] * 2,
        (feat_one, value_one, feat_two, value_two),
        scratch=[
            pltpu.VMEM((2, SHARD, WIDTH), jnp.bfloat16),
            pltpu.SemaphoreType.DMA((4,)),
        ],
        specs=[HBM] * 4,
        vmem=62 << 20,
    )

    two = [own_two] + [fast_shift("row", own_two, -step) for step in range(1, SUB)]
    one = [own_one, fast_swap("col", own_one, 2)]
    one, two = together((jnp.stack(one), jnp.stack(two)))
    one = [one] + [slow_shift("col", one, -step) for step in range(1, SUB)]
    order = (3, 2, 1)
    twos = [two] + [slow_shift("row", two, -step) for step in order]
    one, twos = together((jnp.stack(one, axis=1), twos))
    twos = [twos[0]] + [twos[1 + order.index(step)] for step in range(1, SUB)]
    other = fast_swap("col", one, 1)
    ones = [one[0], one[1], other[0], other[1]]

    def col_scores(*steps):
        kernel = functools.partial(col_kernel, total, scale, len(steps))
        args = (*ones, *(twos[step] for step in steps))
        return call(kernel, [f32(ROWS, BLOCK)] * len(steps), args, work=len(steps) * work)

    def row_scores(ones, twos, halves, weight, *counts):
        shapes = [f32(count, ROWS, BLOCK) for count in counts]
        kernel = functools.partial(row_kernel, total, scale, halves)
        return call(kernel, shapes, (*ones, *twos), work=weight * work)

    def core_merge(mine, theirs, *halves):
        shapes = [f32(ROWS, 2 * SHARD)] * (2 * len(halves))
        return call(functools.partial(core_kernel, halves), shapes, (theirs, mine))

    def spread(axis, parts, first=0):
        return [
            slow_shift(axis, part, first + step) if first + step else part
            for step, part in enumerate(parts)
        ]

    work = BLOCK * BLOCK * SUB
    cols = [None] * SUB
    mine = ones[:2]
    cols[2], cols[3], cols[1] = col_scores(2, 3, 1)
    ones, far = together((ones, cols[1:]))
    (cols[0],) = col_scores(0)
    cols = spread("row", [cols[0], *far])
    (send_one,) = row_scores(ones[2:], twos, ((0, 0), (0, 1)), 2, 2)
    theirs_one = fast_swap("col", send_one, 1)
    (keep_one,) = row_scores(ones[:2], twos, ((0, 0), (0, 1)), 40, 2)
    cols = list(call(block_kernel, [f32(ROWS, SHARD)] * SUB, cols, work=1 * work))
    rows = spread("col", core_merge(keep_one, theirs_one, 0, 1))
    keep, send = call(chip_kernel, [f32(ROWS, SHARD)] * 2, rows)
    theirs = fast_swap("col", send, 2)
    cols[1], keep = together((cols[1], keep))
    cols = [cols[0]] + [fast_shift("row", cols[step], step) for step in range(1, SUB)]
    outs = [f32(SHARD, WIDTH), f32(2, SHARD)] * 2
    return tuple(call(functools.partial(finish_kernel, total), outs, (keep, theirs, *cols)))


def solution(mesh):
    return jax.shard_map(
        body,
        mesh=mesh,
        in_specs=(
            P(("row", "col"), None),
            P(("col", "row"), None),
            P(("row", "col"), None),
            P(("col", "row"), None),
        ),
        out_specs=(
            P(("row", "col"), None),
            P(None, ("row", "col")),
            P(("col", "row"), None),
            P(None, ("col", "row")),
        ),
        check_vma=False,
    )
```

```python
import functools
import math

import jax
import jax.numpy as jnp
from jax import lax
from jax.experimental import pallas as pl
from jax.experimental.pallas import tpu as pltpu
from jax.sharding import PartitionSpec as P

GRID_W = 256
SUB = 4
WAY = (0, 1, 3, 2)
SHARD = 128
WIDTH = 128
BLOCK = SUB * SHARD
ROWS = WIDTH + 8
AUG = 16
TOTAL_ROW, ACROSS_ROW, DOWN_ROW, PEAK_ROW = 0, 1, 2, 3
VMEM = pl.BlockSpec(memory_space=pltpu.VMEM)
HBM = pl.BlockSpec(memory_space=pltpu.HBM)


def slow_shift(axis, value, step):
    pairs = [(i, ((i // SUB + step) % SUB) * SUB + i % SUB) for i in range(SUB * SUB)]
    return lax.ppermute(value, axis, pairs)


def fast_shift(axis, value, step):
    pairs = [(i, (i // SUB) * SUB + (i % SUB + step) % SUB) for i in range(SUB * SUB)]
    return lax.ppermute(value, axis, pairs)


def fast_swap(axis, value, step):
    return lax.ppermute(value, axis, [(i, i ^ step) for i in range(SUB * SUB)])


def pack_kernel(feat_one, value_one, feat_two, value_two, out_one, out_two, held, sems):
    copies = [
        pltpu.make_async_copy(feat_one, out_one.at[:, :WIDTH], sems.at[0]),
        pltpu.make_async_copy(feat_two, out_two.at[:, :WIDTH], sems.at[1]),
        pltpu.make_async_copy(value_one, held.at[0], sems.at[2]),
        pltpu.make_async_copy(value_two, held.at[1], sems.at[3]),
    ]
    for copy in copies:
        copy.start()
    for side, out in ((0, out_one), (1, out_two)):
        copies[2 + side].wait()
        out[:, WIDTH:] = held[side].astype(jnp.float32).T.astype(jnp.bfloat16)
    copies[0].wait()
    copies[1].wait()


def piece_coords(start, total):
    across = (start % GRID_W).astype(jnp.float32) / GRID_W
    down = (start // GRID_W).astype(jnp.float32) / (total // GRID_W)
    return across, down


def coord_rows(start, total):
    across, down = piece_coords(start, total)
    sub = lax.broadcasted_iota(jnp.int32, (AUG, SHARD), 0)
    lane = lax.broadcasted_iota(jnp.int32, (AUG, SHARD), 1).astype(jnp.float32) / GRID_W
    rows = jnp.where(sub == DOWN_ROW, down, 0.0)
    rows = jnp.where(sub == ACROSS_ROW, across + lane, rows)
    rows = jnp.where(sub == TOTAL_ROW, 1.0, rows)
    return rows.astype(jnp.bfloat16)


def block_of(pieces, starts, total):
    keys = jnp.concatenate([piece[:, :WIDTH] for piece in pieces], axis=0)
    values = jnp.concatenate([piece[:, WIDTH:] for piece in pieces], axis=1)
    extra = jnp.concatenate([coord_rows(start, total) for start in starts], axis=1)
    return keys, jnp.concatenate([values, extra], axis=0)


def start_one(slow, fast_high, fast_low):
    row, col = lax.axis_index("row"), lax.axis_index("col")
    x = (col // SUB + slow) % SUB
    fast = (col % SUB) ^ (2 * fast_high + fast_low)
    return ((row * SUB + x) * SUB + fast) * SHARD


def start_two(slow, fast):
    row, col = lax.axis_index("row"), lax.axis_index("col")
    y = (row // SUB + slow) % SUB
    z = (row % SUB + fast) % SUB
    return ((col * SUB + y) * SUB + z) * SHARD


def merge(peaks, parts):
    top = peaks[0]
    for peak in peaks[1:]:
        top = jnp.maximum(top, peak)
    whole = None
    for peak, part in zip(peaks, parts):
        term = part * jnp.exp2(peak - top)
        whole = term if whole is None else whole + term
    return top, whole


def with_peak(top, whole):
    sub = lax.broadcasted_iota(jnp.int32, (ROWS - WIDTH, top.shape[1]), 0)
    return jnp.concatenate(
        [whole[:WIDTH], jnp.where(sub == PEAK_ROW, top, whole[WIDTH:])], axis=0
    )


def peak_of(part):
    return part[WIDTH + PEAK_ROW : WIDTH + PEAK_ROW + 1, :]


def merged(parts):
    return with_peak(*merge([peak_of(part) for part in parts], parts))


def attend(scale, queries, blocks):
    steps = [(tile, block) for tile in range(len(queries)) for block in range(len(blocks))]

    def raw(tile, block):
        return lax.dot_general(
            blocks[block][0],
            queries[tile],
            (((1,), (1,)), ((), ())),
            preferred_element_type=jnp.float32,
        )

    peaks, parts = [[] for _ in queries], [[] for _ in queries]
    ahead = raw(*steps[0])
    for at, (tile, block) in enumerate(steps):
        score = ahead * scale
        if at + 1 < len(steps):
            ahead = raw(*steps[at + 1])
        peak = jnp.max(score, axis=0, keepdims=True)
        weight = jnp.exp2(score - peak).astype(jnp.bfloat16)
        part = jnp.dot(blocks[block][1], weight, preferred_element_type=jnp.float32)
        parts[tile].append(part[:ROWS])
        peaks[tile].append(peak)
    return [with_peak(*merge(*pair)) for pair in zip(peaks, parts)]


def one_block(ones, slow, total):
    pieces = [ones[low * 2 + high][slow] for low in range(2) for high in range(2)]
    starts = [start_one(WAY[slow], high, low) for low in range(2) for high in range(2)]
    return block_of(pieces, starts, total)


def two_block(two, slow, total):
    return block_of(
        [two[piece] for piece in range(SUB)],
        [start_two(slow, WAY[piece]) for piece in range(SUB)],
        total,
    )


def col_kernel(total, scale, count, *refs):
    ones, twos, outs = refs[:SUB], refs[SUB : SUB + count], refs[SUB + count :]
    tiles = [
        jnp.concatenate([two[piece, :, :WIDTH] for piece in range(SUB)], axis=0) for two in twos
    ]
    blocks = [one_block(ones, slow, total) for slow in range(SUB)]
    for out, whole in zip(outs, attend(scale, tiles, blocks)):
        out[...] = whole


def row_kernel(total, scale, halves, *refs):
    ones, twos, outs = refs[:2], refs[2 : 2 + SUB], refs[2 + SUB :]
    tiles = [
        jnp.concatenate(
            [
                ones[2 * core + high][slow, :, :WIDTH]
                for slow in (2 * half, 2 * half + 1)
                for high in range(2)
            ],
            axis=0,
        )
        for core, half in halves
    ]
    blocks = [two_block(two, block, total) for block, two in enumerate(twos)]
    wholes = attend(scale, tiles, blocks)
    for out in outs:
        for index in range(out.shape[0]):
            out[index] = wholes.pop(0)


def core_kernel(halves, *refs):
    (theirs, *mine), outs = refs[: -2 * len(halves)], refs[-2 * len(halves) :]
    for index, half in enumerate(halves):
        own = mine[0][index]
        whole = merged([own, theirs[half]])
        outs[2 * index][...] = whole[:, : 2 * SHARD]
        outs[2 * index + 1][...] = whole[:, 2 * SHARD :]


def chip_kernel(*refs):
    ins, (keep, send) = refs[:SUB], refs[SUB:]
    whole = merged([ref[...] for ref in ins])
    keep[...] = whole[:, :SHARD]
    send[...] = whole[:, SHARD:]


def block_kernel(*refs):
    ins, outs = refs[:SUB], refs[SUB:]
    for piece in range(SUB):
        span = slice(piece * SHARD, (piece + 1) * SHARD)
        outs[piece][...] = merged([ref[:, span] for ref in ins])


def finish_kernel(total, *refs):
    ins, outs = refs[:-4], refs[-4:]
    lane = lax.broadcasted_iota(jnp.int32, (1, SHARD), 1).astype(jnp.float32) / GRID_W
    for side, start in enumerate((start_one(0, 0, 0), start_two(0, 0))):
        matched, flow = outs[2 * side], outs[2 * side + 1]
        own_across, own_down = piece_coords(start, total)
        parts = [ref[...] for ref in (ins[2:] if side else ins[:2])]
        _, whole = merge([peak_of(part) for part in parts], parts)
        inverse = 1.0 / whole[WIDTH + TOTAL_ROW : WIDTH + TOTAL_ROW + 1, :]
        matched[...] = (whole[:WIDTH] * inverse).T
        across = whole[WIDTH + ACROSS_ROW : WIDTH + ACROSS_ROW + 1, :] * inverse
        down = whole[WIDTH + DOWN_ROW : WIDTH + DOWN_ROW + 1, :] * inverse
        flow[0:1, :] = across - (own_across + lane)
        flow[1:2, :] = down - own_down


def call(kernel, shapes, args, scratch=(), work=0, specs=None, vmem=48 << 20):
    moved = sum(math.prod(a.shape) * a.dtype.itemsize for a in (*args, *shapes))
    return pl.pallas_call(
        kernel,
        out_shape=shapes,
        in_specs=specs or [VMEM] * len(args),
        out_specs=[VMEM] * len(shapes),
        scratch_shapes=list(scratch),
        compiler_params=pltpu.CompilerParams(vmem_limit_bytes=vmem),
        cost_estimate=pl.CostEstimate(
            flops=4 * WIDTH * work, bytes_accessed=moved, transcendentals=work
        ),
    )(*args)


def together(values):
    return lax.optimization_barrier(values)


def f32(*shape):
    return jax.ShapeDtypeStruct(shape, jnp.float32)


def bf16(*shape):
    return jax.ShapeDtypeStruct(shape, jnp.bfloat16)


def body(feat_one, feat_two, value_one, value_two):
    total = feat_one.shape[0] * lax.axis_size("row") * lax.axis_size("col")
    scale = math.log2(math.e) / math.sqrt(WIDTH)
    packed = jax.ShapeDtypeStruct((SHARD, 2 * WIDTH), jnp.bfloat16)
    own_one, own_two = call(
        pack_kernel,
        [packed] * 2,
        (feat_one, value_one, feat_two, value_two),
        scratch=[
            pltpu.VMEM((2, SHARD, WIDTH), jnp.bfloat16),
            pltpu.SemaphoreType.DMA((4,)),
        ],
        specs=[HBM] * 4,
        vmem=62 << 20,
    )

    two = [own_two] + [fast_shift("row", own_two, -step) for step in WAY[1:]]
    one = [own_one, fast_swap("col", own_one, 2)]
    one, two = together((jnp.stack(one), jnp.stack(two)))
    one = [one] + [slow_shift("col", one, -step) for step in WAY[1:]]
    order = (2, 3, 1)
    twos = [two] + [slow_shift("row", two, -step) for step in order]
    one, twos = together((jnp.stack(one, axis=1), twos))
    twos = [twos[0]] + [twos[1 + order.index(step)] for step in range(1, SUB)]
    other = fast_swap("col", one, 1)
    ones = [one[0], one[1], other[0], other[1]]

    def col_scores(*steps):
        kernel = functools.partial(col_kernel, total, scale, len(steps))
        args = (*ones, *(twos[step] for step in steps))
        return call(kernel, [f32(ROWS, BLOCK)] * len(steps), args, work=len(steps) * work)

    def row_scores(ones, twos, halves, weight, *counts):
        shapes = [f32(count, ROWS, BLOCK) for count in counts]
        kernel = functools.partial(row_kernel, total, scale, halves)
        return call(kernel, shapes, (*ones, *twos), work=weight * work)

    def core_merge(mine, theirs, *halves):
        shapes = [f32(ROWS, 2 * SHARD)] * (2 * len(halves))
        return call(functools.partial(core_kernel, halves), shapes, (theirs, mine))

    def spread(axis, parts, steps):
        return [
            slow_shift(axis, part, step) if step else part for step, part in zip(steps, parts)
        ]

    work = BLOCK * BLOCK * SUB
    cols = [None] * SUB
    mine = ones[:2]
    cols[2], cols[3], cols[1] = col_scores(2, 3, 1)
    ones, far = together((ones, cols[1:]))
    (cols[0],) = col_scores(0)
    cols = spread("row", [cols[0], *far], range(SUB))
    (send_one,) = row_scores(ones[2:], twos, ((0, 0), (0, 1)), 2, 2)
    theirs_one = fast_swap("col", send_one, 1)
    (keep_one,) = row_scores(ones[:2], twos, ((0, 0), (0, 1)), 40, 2)
    cols = list(call(block_kernel, [f32(ROWS, SHARD)] * SUB, cols, work=1 * work))
    rows = spread("col", core_merge(keep_one, theirs_one, 0, 1), WAY)
    keep, send = call(chip_kernel, [f32(ROWS, SHARD)] * 2, rows)
    theirs = fast_swap("col", send, 2)
    cols[1], keep = together((cols[1], keep))
    cols = [cols[0]] + [fast_shift("row", cols[at], WAY[at]) for at in range(1, SUB)]
    outs = [f32(SHARD, WIDTH), f32(2, SHARD)] * 2
    return tuple(call(functools.partial(finish_kernel, total), outs, (keep, theirs, *cols)))


def solution(mesh):
    return jax.shard_map(
        body,
        mesh=mesh,
        in_specs=(
            P(("row", "col"), None),
            P(("col", "row"), None),
            P(("row", "col"), None),
            P(("col", "row"), None),
        ),
        out_specs=(
            P(("row", "col"), None),
            P(None, ("row", "col")),
            P(("col", "row"), None),
            P(None, ("col", "row")),
        ),
        check_vma=False,
    )
```

```python
import functools
import math

import jax
import jax.numpy as jnp
from jax import lax
from jax.experimental import pallas as pl
from jax.experimental.pallas import tpu as pltpu
from jax.sharding import PartitionSpec as P

GRID_W = 256
SUB = 4
WAY = (0, 1, 3, 2)
SHARD = 128
WIDTH = 128
BLOCK = SUB * SHARD
ROWS = WIDTH + 8
AUG = 16
TOTAL_ROW, ACROSS_ROW, DOWN_ROW, PEAK_ROW = 0, 1, 2, 3
VMEM = pl.BlockSpec(memory_space=pltpu.VMEM)
HBM = pl.BlockSpec(memory_space=pltpu.HBM)


def slow_shift(axis, value, step):
    pairs = [(i, ((i // SUB + step) % SUB) * SUB + i % SUB) for i in range(SUB * SUB)]
    return lax.ppermute(value, axis, pairs)


def fast_shift(axis, value, step):
    pairs = [(i, (i // SUB) * SUB + (i % SUB + step) % SUB) for i in range(SUB * SUB)]
    return lax.ppermute(value, axis, pairs)


def fast_swap(axis, value, step):
    return lax.ppermute(value, axis, [(i, i ^ step) for i in range(SUB * SUB)])


def pack_kernel(feat_one, value_one, feat_two, value_two, out_one, out_two, held, sems):
    copies = [
        pltpu.make_async_copy(feat_one, out_one.at[:, :WIDTH], sems.at[0]),
        pltpu.make_async_copy(feat_two, out_two.at[:, :WIDTH], sems.at[1]),
        pltpu.make_async_copy(value_one, held.at[0], sems.at[2]),
        pltpu.make_async_copy(value_two, held.at[1], sems.at[3]),
    ]
    for copy in copies:
        copy.start()
    for side, out in ((0, out_one), (1, out_two)):
        copies[2 + side].wait()
        out[:, WIDTH:] = held[side].astype(jnp.float32).T.astype(jnp.bfloat16)
    copies[0].wait()
    copies[1].wait()


def piece_coords(start, total):
    across = (start % GRID_W).astype(jnp.float32) / GRID_W
    down = (start // GRID_W).astype(jnp.float32) / (total // GRID_W)
    return across, down


def coord_rows(start, total):
    across, down = piece_coords(start, total)
    sub = lax.broadcasted_iota(jnp.int32, (AUG, SHARD), 0)
    lane = lax.broadcasted_iota(jnp.int32, (AUG, SHARD), 1).astype(jnp.float32) / GRID_W
    rows = jnp.where(sub == DOWN_ROW, down, 0.0)
    rows = jnp.where(sub == ACROSS_ROW, across + lane, rows)
    rows = jnp.where(sub == TOTAL_ROW, 1.0, rows)
    return rows.astype(jnp.bfloat16)


def block_of(pieces, starts, total):
    keys = jnp.concatenate([piece[:, :WIDTH] for piece in pieces], axis=0)
    values = jnp.concatenate([piece[:, WIDTH:] for piece in pieces], axis=1)
    extra = jnp.concatenate([coord_rows(start, total) for start in starts], axis=1)
    return keys, jnp.concatenate([values, extra], axis=0)


def start_one(slow, fast_high, fast_low):
    row, col = lax.axis_index("row"), lax.axis_index("col")
    x = (col // SUB + slow) % SUB
    fast = (col % SUB) ^ (2 * fast_high + fast_low)
    return ((row * SUB + x) * SUB + fast) * SHARD


def start_two(slow, fast):
    row, col = lax.axis_index("row"), lax.axis_index("col")
    y = (row // SUB + slow) % SUB
    z = (row % SUB + fast) % SUB
    return ((col * SUB + y) * SUB + z) * SHARD


def merge(peaks, parts):
    top = peaks[0]
    for peak in peaks[1:]:
        top = jnp.maximum(top, peak)
    whole = None
    for peak, part in zip(peaks, parts):
        term = part * jnp.exp2(peak - top)
        whole = term if whole is None else whole + term
    return top, whole


def with_peak(top, whole):
    sub = lax.broadcasted_iota(jnp.int32, (ROWS - WIDTH, top.shape[1]), 0)
    return jnp.concatenate(
        [whole[:WIDTH], jnp.where(sub == PEAK_ROW, top, whole[WIDTH:])], axis=0
    )


def peak_of(part):
    return part[WIDTH + PEAK_ROW : WIDTH + PEAK_ROW + 1, :]


def merged(parts):
    return with_peak(*merge([peak_of(part) for part in parts], parts))


def attend(scale, queries, blocks):
    steps = [(tile, block) for tile in range(len(queries)) for block in range(len(blocks))]

    def raw(tile, block):
        return lax.dot_general(
            blocks[block][0],
            queries[tile],
            (((1,), (1,)), ((), ())),
            preferred_element_type=jnp.float32,
        )

    peaks, parts = [[] for _ in queries], [[] for _ in queries]
    ahead = raw(*steps[0])
    for at, (tile, block) in enumerate(steps):
        score = ahead * scale
        if at + 1 < len(steps):
            ahead = raw(*steps[at + 1])
        peak = jnp.max(score, axis=0, keepdims=True)
        weight = jnp.exp2(score - peak).astype(jnp.bfloat16)
        part = jnp.dot(blocks[block][1], weight, preferred_element_type=jnp.float32)
        parts[tile].append(part[:ROWS])
        peaks[tile].append(peak)
    return [with_peak(*merge(*pair)) for pair in zip(peaks, parts)]


def one_block(ones, slow, total):
    pieces = [ones[low * 2 + high][slow] for low in range(2) for high in range(2)]
    starts = [start_one(slow, high, low) for low in range(2) for high in range(2)]
    return block_of(pieces, starts, total)


def two_block(two, slow, total):
    return block_of(
        [two[piece] for piece in range(SUB)],
        [start_two(slow, WAY[piece]) for piece in range(SUB)],
        total,
    )


def col_kernel(total, scale, count, *refs):
    ones, twos, outs = refs[:SUB], refs[SUB : SUB + count], refs[SUB + count :]
    tiles = [
        jnp.concatenate([two[piece, :, :WIDTH] for piece in range(SUB)], axis=0) for two in twos
    ]
    blocks = [one_block(ones, slow, total) for slow in range(SUB)]
    for out, whole in zip(outs, attend(scale, tiles, blocks)):
        out[...] = whole


def row_kernel(total, scale, halves, *refs):
    ones, twos, outs = refs[:2], refs[2 : 2 + SUB], refs[2 + SUB :]
    tiles = [
        jnp.concatenate(
            [
                ones[2 * core + high][slow, :, :WIDTH]
                for slow in (2 * half, 2 * half + 1)
                for high in range(2)
            ],
            axis=0,
        )
        for core, half in halves
    ]
    blocks = [two_block(two, block, total) for block, two in enumerate(twos)]
    wholes = attend(scale, tiles, blocks)
    for out in outs:
        for index in range(out.shape[0]):
            out[index] = wholes.pop(0)


def core_kernel(halves, *refs):
    (theirs, *mine), outs = refs[: -2 * len(halves)], refs[-2 * len(halves) :]
    for index, half in enumerate(halves):
        own = mine[0][index]
        whole = merged([own, theirs[half]])
        outs[2 * index][...] = whole[:, : 2 * SHARD]
        outs[2 * index + 1][...] = whole[:, 2 * SHARD :]


def chip_kernel(*refs):
    ins, (keep, send) = refs[:SUB], refs[SUB:]
    whole = merged([ref[...] for ref in ins])
    keep[...] = whole[:, :SHARD]
    send[...] = whole[:, SHARD:]


def block_kernel(*refs):
    ins, outs = refs[:SUB], refs[SUB:]
    for piece in range(SUB):
        span = slice(piece * SHARD, (piece + 1) * SHARD)
        outs[piece][...] = merged([ref[:, span] for ref in ins])


def finish_kernel(total, *refs):
    ins, outs = refs[:-4], refs[-4:]
    lane = lax.broadcasted_iota(jnp.int32, (1, SHARD), 1).astype(jnp.float32) / GRID_W
    for side, start in enumerate((start_one(0, 0, 0), start_two(0, 0))):
        matched, flow = outs[2 * side], outs[2 * side + 1]
        own_across, own_down = piece_coords(start, total)
        parts = [ref[...] for ref in (ins[2:] if side else ins[:2])]
        _, whole = merge([peak_of(part) for part in parts], parts)
        inverse = 1.0 / whole[WIDTH + TOTAL_ROW : WIDTH + TOTAL_ROW + 1, :]
        matched[...] = (whole[:WIDTH] * inverse).T
        across = whole[WIDTH + ACROSS_ROW : WIDTH + ACROSS_ROW + 1, :] * inverse
        down = whole[WIDTH + DOWN_ROW : WIDTH + DOWN_ROW + 1, :] * inverse
        flow[0:1, :] = across - (own_across + lane)
        flow[1:2, :] = down - own_down


def call(kernel, shapes, args, scratch=(), work=0, specs=None, vmem=48 << 20):
    moved = sum(math.prod(a.shape) * a.dtype.itemsize for a in (*args, *shapes))
    return pl.pallas_call(
        kernel,
        out_shape=shapes,
        in_specs=specs or [VMEM] * len(args),
        out_specs=[VMEM] * len(shapes),
        scratch_shapes=list(scratch),
        compiler_params=pltpu.CompilerParams(vmem_limit_bytes=vmem),
        cost_estimate=pl.CostEstimate(
            flops=4 * WIDTH * work, bytes_accessed=moved, transcendentals=work
        ),
    )(*args)


def together(values):
    return lax.optimization_barrier(values)


def f32(*shape):
    return jax.ShapeDtypeStruct(shape, jnp.float32)


def bf16(*shape):
    return jax.ShapeDtypeStruct(shape, jnp.bfloat16)


def body(feat_one, feat_two, value_one, value_two):
    total = feat_one.shape[0] * lax.axis_size("row") * lax.axis_size("col")
    scale = math.log2(math.e) / math.sqrt(WIDTH)
    packed = jax.ShapeDtypeStruct((SHARD, 2 * WIDTH), jnp.bfloat16)
    own_one, own_two = call(
        pack_kernel,
        [packed] * 2,
        (feat_one, value_one, feat_two, value_two),
        scratch=[
            pltpu.VMEM((2, SHARD, WIDTH), jnp.bfloat16),
            pltpu.SemaphoreType.DMA((4,)),
        ],
        specs=[HBM] * 4,
        vmem=62 << 20,
    )

    two = [own_two] + [fast_shift("row", own_two, -step) for step in WAY[1:]]
    one = [own_one, fast_swap("col", own_one, 2)]
    one, two = together((jnp.stack(one), jnp.stack(two)))
    one = [one] + [slow_shift("col", one, -step) for step in range(1, SUB)]
    order = (3, 2, 1)
    twos = [two] + [slow_shift("row", two, -step) for step in order]
    one, twos = together((jnp.stack(one, axis=1), twos))
    twos = [twos[0]] + [twos[1 + order.index(step)] for step in range(1, SUB)]
    other = fast_swap("col", one, 1)
    ones = [one[0], one[1], other[0], other[1]]

    def col_scores(*steps):
        kernel = functools.partial(col_kernel, total, scale, len(steps))
        args = (*ones, *(twos[step] for step in steps))
        return call(kernel, [f32(ROWS, BLOCK)] * len(steps), args, work=len(steps) * work)

    def row_scores(ones, twos, halves, weight, *counts):
        shapes = [f32(count, ROWS, BLOCK) for count in counts]
        kernel = functools.partial(row_kernel, total, scale, halves)
        return call(kernel, shapes, (*ones, *twos), work=weight * work)

    def core_merge(mine, theirs, *halves):
        shapes = [f32(ROWS, 2 * SHARD)] * (2 * len(halves))
        return call(functools.partial(core_kernel, halves), shapes, (theirs, mine))

    def spread(axis, parts, steps):
        return [
            slow_shift(axis, part, step) if step else part for step, part in zip(steps, parts)
        ]

    work = BLOCK * BLOCK * SUB
    cols = [None] * SUB
    mine = ones[:2]
    cols[2], cols[3], cols[1] = col_scores(2, 3, 1)
    ones, far = together((ones, cols[1:]))
    (cols[0],) = col_scores(0)
    cols = spread("row", [cols[0], *far], range(SUB))
    (send_one,) = row_scores(ones[2:], twos, ((0, 0), (0, 1)), 2, 2)
    theirs_one = fast_swap("col", send_one, 1)
    (keep_one,) = row_scores(ones[:2], twos, ((0, 0), (0, 1)), 40, 2)
    cols = list(call(block_kernel, [f32(ROWS, SHARD)] * SUB, cols, work=1 * work))
    rows = spread("col", core_merge(keep_one, theirs_one, 0, 1), range(SUB))
    keep, send = call(chip_kernel, [f32(ROWS, SHARD)] * 2, rows)
    theirs = fast_swap("col", send, 2)
    cols[1], keep = together((cols[1], keep))
    cols = [cols[0]] + [fast_shift("row", cols[at], WAY[at]) for at in range(1, SUB)]
    outs = [f32(SHARD, WIDTH), f32(2, SHARD)] * 2
    return tuple(call(functools.partial(finish_kernel, total), outs, (keep, theirs, *cols)))


def solution(mesh):
    return jax.shard_map(
        body,
        mesh=mesh,
        in_specs=(
            P(("row", "col"), None),
            P(("col", "row"), None),
            P(("row", "col"), None),
            P(("col", "row"), None),
        ),
        out_specs=(
            P(("row", "col"), None),
            P(None, ("row", "col")),
            P(("col", "row"), None),
            P(None, ("col", "row")),
        ),
        check_vma=False,
    )
```

```python
import functools
import math

import jax
import jax.numpy as jnp
from jax import lax
from jax.experimental import pallas as pl
from jax.experimental.pallas import tpu as pltpu
from jax.sharding import PartitionSpec as P

GRID_W = 256
SUB = 4
SHARD = 128
WIDTH = 128
BLOCK = SUB * SHARD
ROWS = WIDTH + 8
AUG = 16
TOTAL_ROW, ACROSS_ROW, DOWN_ROW, PEAK_ROW = 0, 1, 2, 3
VMEM = pl.BlockSpec(memory_space=pltpu.VMEM)
HBM = pl.BlockSpec(memory_space=pltpu.HBM)


def slow_shift(axis, value, step):
    pairs = [(i, ((i // SUB + step) % SUB) * SUB + i % SUB) for i in range(SUB * SUB)]
    return lax.ppermute(value, axis, pairs)


def fast_shift(axis, value, step):
    pairs = [(i, (i // SUB) * SUB + (i % SUB + step) % SUB) for i in range(SUB * SUB)]
    return lax.ppermute(value, axis, pairs)


def fast_swap(axis, value, step):
    return lax.ppermute(value, axis, [(i, i ^ step) for i in range(SUB * SUB)])


def pack_kernel(feat_one, value_one, feat_two, value_two, out_one, out_two, held, sems):
    copies = [
        pltpu.make_async_copy(feat_one, out_one.at[:, :WIDTH], sems.at[0]),
        pltpu.make_async_copy(feat_two, out_two.at[:, :WIDTH], sems.at[1]),
        pltpu.make_async_copy(value_one, held.at[0], sems.at[2]),
        pltpu.make_async_copy(value_two, held.at[1], sems.at[3]),
    ]
    for copy in copies:
        copy.start()
    for side, out in ((0, out_one), (1, out_two)):
        copies[2 + side].wait()
        out[:, WIDTH:] = held[side].astype(jnp.float32).T.astype(jnp.bfloat16)
    copies[0].wait()
    copies[1].wait()


def piece_coords(start, total):
    across = (start % GRID_W).astype(jnp.float32) / GRID_W
    down = (start // GRID_W).astype(jnp.float32) / (total // GRID_W)
    return across, down


def coord_rows(start, total):
    across, down = piece_coords(start, total)
    sub = lax.broadcasted_iota(jnp.int32, (AUG, SHARD), 0)
    lane = lax.broadcasted_iota(jnp.int32, (AUG, SHARD), 1).astype(jnp.float32) / GRID_W
    rows = jnp.where(sub == DOWN_ROW, down, 0.0)
    rows = jnp.where(sub == ACROSS_ROW, across + lane, rows)
    rows = jnp.where(sub == TOTAL_ROW, 1.0, rows)
    return rows.astype(jnp.bfloat16)


def block_of(pieces, starts, total):
    keys = jnp.concatenate([piece[:, :WIDTH] for piece in pieces], axis=0)
    values = jnp.concatenate([piece[:, WIDTH:] for piece in pieces], axis=1)
    extra = jnp.concatenate([coord_rows(start, total) for start in starts], axis=1)
    return keys, jnp.concatenate([values, extra], axis=0)


def start_one(slow, fast_high, fast_low):
    row, col = lax.axis_index("row"), lax.axis_index("col")
    x = (col // SUB + slow) % SUB
    fast = (col % SUB) ^ (2 * fast_high + fast_low)
    return ((row * SUB + x) * SUB + fast) * SHARD


def start_two(slow, fast):
    row, col = lax.axis_index("row"), lax.axis_index("col")
    y = (row // SUB + slow) % SUB
    z = (row % SUB + fast) % SUB
    return ((col * SUB + y) * SUB + z) * SHARD


def merge(peaks, parts):
    top = peaks[0]
    for peak in peaks[1:]:
        top = jnp.maximum(top, peak)
    whole = None
    for peak, part in zip(peaks, parts):
        term = part * jnp.exp2(peak - top)
        whole = term if whole is None else whole + term
    return top, whole


def with_peak(top, whole):
    sub = lax.broadcasted_iota(jnp.int32, (ROWS - WIDTH, top.shape[1]), 0)
    return jnp.concatenate(
        [whole[:WIDTH], jnp.where(sub == PEAK_ROW, top, whole[WIDTH:])], axis=0
    )


def peak_of(part):
    return part[WIDTH + PEAK_ROW : WIDTH + PEAK_ROW + 1, :]


def merged(parts):
    return with_peak(*merge([peak_of(part) for part in parts], parts))


def attend(scale, queries, blocks):
    steps = [(tile, block) for tile in range(len(queries)) for block in range(len(blocks))]

    def raw(tile, block):
        return lax.dot_general(
            blocks[block][0],
            queries[tile],
            (((1,), (1,)), ((), ())),
            preferred_element_type=jnp.float32,
        )

    peaks, parts = [[] for _ in queries], [[] for _ in queries]
    ahead = raw(*steps[0])
    for at, (tile, block) in enumerate(steps):
        score = ahead * scale
        if at + 1 < len(steps):
            ahead = raw(*steps[at + 1])
        peak = jnp.max(score, axis=0, keepdims=True)
        weight = jnp.exp2(score - peak).astype(jnp.bfloat16)
        part = jnp.dot(blocks[block][1], weight, preferred_element_type=jnp.float32)
        parts[tile].append(part[:ROWS])
        peaks[tile].append(peak)
    return [with_peak(*merge(*pair)) for pair in zip(peaks, parts)]


def one_block(ones, slow, total):
    pieces = [ones[low * 2 + high][slow] for low in range(2) for high in range(2)]
    starts = [start_one(slow, high, low) for low in range(2) for high in range(2)]
    return block_of(pieces, starts, total)


def two_block(two, slow, total):
    return block_of(
        [two[piece] for piece in range(SUB)],
        [start_two(slow, piece) for piece in range(SUB)],
        total,
    )


def col_kernel(total, scale, count, *refs):
    ones, twos, outs = refs[:SUB], refs[SUB : SUB + count], refs[SUB + count :]
    tiles = [
        jnp.concatenate([two[piece, :, :WIDTH] for piece in range(SUB)], axis=0) for two in twos
    ]
    blocks = [one_block(ones, slow, total) for slow in range(SUB)]
    for out, whole in zip(outs, attend(scale, tiles, blocks)):
        out[...] = whole


def row_kernel(total, scale, halves, *refs):
    ones, twos, outs = refs[:2], refs[2 : 2 + SUB], refs[2 + SUB :]
    tiles = [
        jnp.concatenate(
            [
                ones[2 * core + high][slow, :, :WIDTH]
                for slow in (2 * half, 2 * half + 1)
                for high in range(2)
            ],
            axis=0,
        )
        for core, half in halves
    ]
    blocks = [two_block(two, block, total) for block, two in enumerate(twos)]
    wholes = attend(scale, tiles, blocks)
    for out in outs:
        for index in range(out.shape[0]):
            out[index] = wholes.pop(0)


def core_kernel(halves, *refs):
    (theirs, *mine), outs = refs[: -2 * len(halves)], refs[-2 * len(halves) :]
    for index, half in enumerate(halves):
        own = mine[0][index]
        whole = merged([own, theirs[half]])
        outs[2 * index][...] = whole[:, : 2 * SHARD]
        outs[2 * index + 1][...] = whole[:, 2 * SHARD :]


def chip_kernel(*refs):
    ins, (keep, send) = refs[:SUB], refs[SUB:]
    whole = merged([ref[...] for ref in ins])
    keep[...] = whole[:, :SHARD]
    send[...] = whole[:, SHARD:]


def block_kernel(*refs):
    ins, outs = refs[:SUB], refs[SUB:]
    for piece in range(SUB):
        span = slice(piece * SHARD, (piece + 1) * SHARD)
        outs[piece][...] = merged([ref[:, span] for ref in ins])


def finish_kernel(total, *refs):
    ins, outs = refs[:-4], refs[-4:]
    lane = lax.broadcasted_iota(jnp.int32, (1, SHARD), 1).astype(jnp.float32) / GRID_W
    for side, start in enumerate((start_one(0, 0, 0), start_two(0, 0))):
        matched, flow = outs[2 * side], outs[2 * side + 1]
        own_across, own_down = piece_coords(start, total)
        parts = [ref[...] for ref in (ins[2:] if side else ins[:2])]
        _, whole = merge([peak_of(part) for part in parts], parts)
        inverse = 1.0 / whole[WIDTH + TOTAL_ROW : WIDTH + TOTAL_ROW + 1, :]
        matched[...] = (whole[:WIDTH] * inverse).T
        across = whole[WIDTH + ACROSS_ROW : WIDTH + ACROSS_ROW + 1, :] * inverse
        down = whole[WIDTH + DOWN_ROW : WIDTH + DOWN_ROW + 1, :] * inverse
        flow[0:1, :] = across - (own_across + lane)
        flow[1:2, :] = down - own_down


def call(kernel, shapes, args, scratch=(), work=0, specs=None, vmem=48 << 20):
    moved = sum(math.prod(a.shape) * a.dtype.itemsize for a in (*args, *shapes))
    return pl.pallas_call(
        kernel,
        out_shape=shapes,
        in_specs=specs or [VMEM] * len(args),
        out_specs=[VMEM] * len(shapes),
        scratch_shapes=list(scratch),
        compiler_params=pltpu.CompilerParams(vmem_limit_bytes=vmem),
        cost_estimate=pl.CostEstimate(
            flops=4 * WIDTH * work, bytes_accessed=moved, transcendentals=work
        ),
    )(*args)


def together(values):
    return lax.optimization_barrier(values)


def f32(*shape):
    return jax.ShapeDtypeStruct(shape, jnp.float32)


def bf16(*shape):
    return jax.ShapeDtypeStruct(shape, jnp.bfloat16)


def body(feat_one, feat_two, value_one, value_two):
    total = feat_one.shape[0] * lax.axis_size("row") * lax.axis_size("col")
    scale = math.log2(math.e) / math.sqrt(WIDTH)
    packed = jax.ShapeDtypeStruct((SHARD, 2 * WIDTH), jnp.bfloat16)
    own_one, own_two = call(
        pack_kernel,
        [packed] * 2,
        (feat_one, value_one, feat_two, value_two),
        scratch=[
            pltpu.VMEM((2, SHARD, WIDTH), jnp.bfloat16),
            pltpu.SemaphoreType.DMA((4,)),
        ],
        specs=[HBM] * 4,
        vmem=62 << 20,
    )

    two = [own_two] + [fast_shift("row", own_two, -step) for step in range(1, SUB)]
    one = [own_one, fast_swap("col", own_one, 2)]
    one, two = together((jnp.stack(one), jnp.stack(two)))
    one = [one] + [slow_shift("col", one, -step) for step in range(1, SUB)]
    order = (3, 2, 1)
    twos = [two] + [slow_shift("row", two, -step) for step in order]
    one, twos = together((jnp.stack(one, axis=1), twos))
    twos = [twos[0]] + [twos[1 + order.index(step)] for step in range(1, SUB)]
    other = fast_swap("col", one, 1)
    ones = [one[0], one[1], other[0], other[1]]

    def col_scores(*steps):
        kernel = functools.partial(col_kernel, total, scale, len(steps))
        args = (*ones, *(twos[step] for step in steps))
        return call(kernel, [f32(ROWS, BLOCK)] * len(steps), args, work=len(steps) * work)

    def row_scores(ones, twos, halves, weight, *counts):
        shapes = [f32(count, ROWS, BLOCK) for count in counts]
        kernel = functools.partial(row_kernel, total, scale, halves)
        return call(kernel, shapes, (*ones, *twos), work=weight * work)

    def core_merge(mine, theirs, *halves):
        shapes = [f32(ROWS, 2 * SHARD)] * (2 * len(halves))
        return call(functools.partial(core_kernel, halves), shapes, (theirs, mine))

    def spread(axis, parts, first=0):
        return [
            slow_shift(axis, part, first + step) if first + step else part
            for step, part in enumerate(parts)
        ]

    work = BLOCK * BLOCK * SUB
    cols = [None] * SUB
    mine = ones[:2]
    cols[2], cols[3], cols[1] = col_scores(2, 3, 1)
    ones, far = together((ones, cols[1:]))
    (cols[0],) = col_scores(0)
    cols = spread("row", [cols[0], *far])
    (send_one,) = row_scores(ones[2:], twos, ((0, 0), (0, 1)), 2, 2)
    theirs_one = fast_swap("col", send_one, 1)
    (keep_one,) = row_scores(ones[:2], twos, ((0, 0), (0, 1)), 40, 2)
    cols = list(call(block_kernel, [f32(ROWS, SHARD)] * SUB, cols, work=1 * work))
    rows = spread("col", core_merge(keep_one, theirs_one, 0, 1))
    keep, send = call(chip_kernel, [f32(ROWS, SHARD)] * 2, rows)
    theirs = fast_swap("col", send, 2)
    cols[1], cols[3], keep = together((cols[1], cols[3], keep))
    cols = [cols[0]] + [fast_shift("row", cols[step], step) for step in range(1, SUB)]
    outs = [f32(SHARD, WIDTH), f32(2, SHARD)] * 2
    return tuple(call(functools.partial(finish_kernel, total), outs, (keep, theirs, *cols)))


def solution(mesh):
    return jax.shard_map(
        body,
        mesh=mesh,
        in_specs=(
            P(("row", "col"), None),
            P(("col", "row"), None),
            P(("row", "col"), None),
            P(("col", "row"), None),
        ),
        out_specs=(
            P(("row", "col"), None),
            P(None, ("row", "col")),
            P(("col", "row"), None),
            P(None, ("col", "row")),
        ),
        check_vma=False,
    )
```
